128 devices in a mesh: az: 16 (over z_hi, y, core), gz: 8 (over x, z_lo).
Axes of the slice: x: 4, y: 4, z: 4 (z_hi: 2, z_lo: 2; z = z_hi * 2 + z_lo), core: 2. Of those that a mesh axis runs over, the one named last changes fastest.
Arguments:
- starting_warmth: float32 [128, 512, 1024], P(None, 'az', 'gz'), may hold values from -6 to 6
- volume_transfer_multiplier: float32 [128, 512, 1024], P(None, 'az', 'gz'), may hold values from 0.005 to 4
- energy_supply_history: float32 [128, 512, 1024], P(None, 'az', 'gz'), may hold values from -1 to 2
Outputs:
- final_temperature: float32 [128, 512, 1024], P(None, 'az', 'gz')
The draws below stay inside these ranges and needn't reach their ends.
All inputs are finite; a program needn't handle non-finite values.
Results may differ from the reference program's by a relative error of at most 0.0003.
Values sent between devices are 32-bit elements; how exact they have to be, the bound alone decides.
A program may use at most 128 MiB of HBM per device.

```python
import math
import jax
import jax.numpy as jnp
from jax import lax

ANGULAR_SIZE = 512
OUTWARD_SIZE = 128
STEPS = 2
PICARD = 2
LENGTHWISE_SIZE = 1024


def draw_volume_transfer_multiplier(key, part):
    array_shape = (OUTWARD_SIZE, ANGULAR_SIZE, LENGTHWISE_SIZE)
    base_key = jax.random.fold_in(key, 11)
    pick_key = jax.random.fold_in(key, 12)
    weak_key = jax.random.fold_in(key, 13)
    base_values = jnp.exp(jax.random.uniform(base_key, array_shape, jnp.float32, math.log(0.5), math.log(4.0)))
    weak_values = jnp.exp(jax.random.uniform(weak_key, array_shape, jnp.float32, math.log(0.005), math.log(0.05)))
    picked_cells = jax.random.uniform(pick_key, array_shape, jnp.float32) < 1.0 / 128.0
    return jnp.where(picked_cells, weak_values, base_values).astype(jnp.float32)


def levels(own_key, extent, pieces, smallest, top_value):
    loudness, own = 1.0, jax.random.fold_in(own_key, 6)
    for axis_at, parts in pieces:
        draws = jnp.exp(jax.random.uniform(jax.random.fold_in(own, axis_at), (parts,), jnp.float32, smallest / len(pieces), top_value / len(pieces)))
        loudness = loudness * jnp.repeat(draws, extent[axis_at] // parts).reshape([-1 if axis == axis_at else 1 for axis in range(len(extent))])
    return loudness


def centred(stream_key, extent, spread, limit, shards=(), kind=jnp.bfloat16):
    gain = levels(stream_key, extent, shards, -0.22, 0.18) if shards else 1.0
    entries = jax.random.normal(stream_key, extent, jnp.float32) * spread * gain
    return jnp.minimum(jnp.maximum(entries, -limit), limit).astype(kind)


def setup_inputs(seed: int = 0) -> dict:
    seeds = jax.random.split(jax.random.key(seed), 4)
    starting_warmth = centred(seeds[0], (OUTWARD_SIZE, ANGULAR_SIZE, LENGTHWISE_SIZE), 1.0, 6.0, ((1, 16), (2, 8)), jnp.float32)
    volume_transfer_multiplier = draw_volume_transfer_multiplier(jax.random.fold_in(seeds[3], 71), 0)
    energy_supply_history = jnp.clip(-1.0 + 3.0 * jax.random.uniform(seeds[2], (OUTWARD_SIZE, ANGULAR_SIZE, LENGTHWISE_SIZE), jnp.float32) ** levels(seeds[2], (OUTWARD_SIZE, ANGULAR_SIZE, LENGTHWISE_SIZE), ((1, 16), (2, 8)), -0.2, 0.2), -1.0, 2.0)
    return dict(starting_warmth=starting_warmth, volume_transfer_multiplier=volume_transfer_multiplier, energy_supply_history=energy_supply_history)


diffusion_number = 1000.0
lengthwise_ratio = 0.048


def transfer_coefficient(field_values, starting_entries):
    return starting_entries * (1.5 + jnp.tanh(field_values))


def harmonic(first_value, second_value):
    return 2.0 * first_value * second_value / (first_value + second_value)


def thomas(lower_band, middle_band, upper_band, right_side):
    def forward(carry, row):
        carry_prev, solve_prev = carry
        low_row, mid_row, up_row, rhs_row = row
        pivot_row = mid_row - low_row * carry_prev
        carry_next = up_row / pivot_row
        solve_next = (rhs_row - low_row[None] * solve_prev) / pivot_row[None]
        return (carry_next, solve_next), (carry_next, solve_next)

    start = (jnp.zeros_like(middle_band[0]), jnp.zeros_like(right_side[0]))
    final_state, (carries, partial_value) = lax.scan(forward, start, (lower_band, middle_band, upper_band, right_side))

    def backward(later, row):
        carry_row, part_row = row
        value = part_row - carry_row[None] * later
        return value, value

    final_back, solved = lax.scan(backward, jnp.zeros_like(right_side[0]), (carries, partial_value), reverse=True)
    return solved


def cyclic_solve(lower_band, middle_band, upper_band, right_side):
    count = middle_band.shape[0]
    shape_tail = (1,) * (right_side.ndim - 1)
    positions = jnp.arange(count - 1).reshape((count - 1,) + shape_tail)
    first_mask = (positions == 0).astype(right_side.dtype)
    last_mask = (positions == count - 2).astype(right_side.dtype)
    border = first_mask * (-lower_band[1])[None] + last_mask * (-upper_band[count - 1])[None]
    stacked = jnp.stack([right_side[1:], border], axis=1)
    solved = thomas(lower_band[1:], middle_band[1:], upper_band[1:], stacked)
    base_part = solved[:, 0]
    unit_part = solved[:, 1]
    head_value = (right_side[0] - lower_band[0] * base_part[-1] - upper_band[0] * base_part[0]) / (
        middle_band[0] + lower_band[0] * unit_part[-1] + upper_band[0] * unit_part[0])
    return jnp.concatenate([head_value[None], base_part + unit_part * head_value[None]], axis=0)


def lengthwise_spacing(warmth_mesh, starting_entries, energy_supply_history):
    thermal_coupling = transfer_coefficient(warmth_mesh, starting_entries)
    empty_sheet = jnp.zeros_like(warmth_mesh[:, :, :1])
    upper_warmth = jnp.concatenate([warmth_mesh[:, :, 1:], empty_sheet], axis=2)
    lower_warmth = jnp.concatenate([empty_sheet, warmth_mesh[:, :, :-1]], axis=2)
    above_cond = jnp.concatenate([thermal_coupling[:, :, 1:], empty_sheet], axis=2)
    below_cond = jnp.concatenate([empty_sheet, thermal_coupling[:, :, :-1]], axis=2)
    upper_surface = harmonic(thermal_coupling, above_cond)
    lower_surface = harmonic(thermal_coupling, below_cond)
    return warmth_mesh + lengthwise_ratio * (upper_surface * (upper_warmth - warmth_mesh) - lower_surface * (warmth_mesh - lower_warmth)) + energy_supply_history


def reference(starting_warmth, volume_transfer_multiplier, energy_supply_history):
    radius_rows = jnp.arange(OUTWARD_SIZE).astype(jnp.float32)
    number = (diffusion_number * (OUTWARD_SIZE / (OUTWARD_SIZE + radius_rows)) ** 2)[None, :, None]
    base_moved = jnp.moveaxis(volume_transfer_multiplier, 1, 0)
    warmth_mesh = starting_warmth
    for time_step in range(STEPS):
        forward_estimate = lengthwise_spacing(warmth_mesh, volume_transfer_multiplier, energy_supply_history)
        desired_outcome = jnp.moveaxis(forward_estimate, 1, 0)
        trial_profile = desired_outcome
        for picard_sweep in range(PICARD):
            thermal_coupling = transfer_coefficient(trial_profile, base_moved)
            face_values = harmonic(thermal_coupling, jnp.roll(thermal_coupling, -1, axis=0))
            behind = jnp.roll(face_values, 1, axis=0)
            lower_band = -number * behind
            upper_band = -number * face_values
            middle_band = 1.0 + number * (behind + face_values)
            trial_profile = cyclic_solve(lower_band, middle_band, upper_band, desired_outcome)
        warmth_mesh = jnp.moveaxis(trial_profile, 0, 1)
    return warmth_mesh
```

```python
import functools

import jax
import jax.numpy as jnp
from jax import lax
from jax.experimental import pallas as pl
from jax.experimental.pallas import tpu as pltpu
from jax.sharding import PartitionSpec as P

STEPS = 2
PICARD = 2
diffusion_number = 1000.0
lengthwise_ratio = 0.048

MESH = pl.DeviceIdType.MESH
CELLS = 64
HALF = 32
ROWS = 64
TILES = 8
LANES = 128
VALUES = 7
STARTS = (0, 16, 32, 48)
ENDS = (16, 32, 48, 63)


def row_block(tile):
    return pl.ds(pl.multiple_of(tile * 8, 8), 8)


def conduct(field, factor):
    return factor * (1.5 + jnp.tanh(field))


def eliminate(ground, left, right, side):
    inverse = 1.0 / (ground + left + right)
    to_left = left * inverse
    to_right = right * inverse
    return to_left, to_right, side * inverse


def kernel(
    warmth_hbm, factor_hbm, supply_hbm, out_hbm,
    field, factor, supply, goal, to_sep, to_next, base, stage,
    ends, factor_ends, near_ends, near_factor,
    packet, gathered, answer, returned,
    own_sem, stage_sem, swap_send, swap_recv, halo_send, halo_recv,
    packet_send, packet_recv, answer_send, answer_recv, out_sem, out_send, out_recv,
):
    az = lax.axis_index("az")
    gz = lax.axis_index("gz")
    core = lax.rem(az, 2)
    chip = az // 2
    sibling = az + 1 - 2 * core
    gz_count = lax.axis_size("gz")
    across = gz + 1 - 2 * lax.rem(gz, 2)
    gz_up = lax.rem(gz + 1, gz_count)
    gz_down = lax.rem(gz + gz_count - 1, gz_count)
    other = lax.rem(gz + gz_count - 1 + 2 * lax.rem(gz, 2), gz_count)

    barrier = pltpu.get_barrier_semaphore()
    for member in range(TILES):
        pl.semaphore_signal(
            barrier, inc=1, device_id=(2 * member + core, across), device_id_type=MESH
        )
    pl.semaphore_signal(barrier, inc=1, device_id=(sibling, gz), device_id_type=MESH)
    pl.semaphore_signal(barrier, inc=1, device_id=(az, other), device_id_type=MESH)

    arrays = ((warmth_hbm, field), (factor_hbm, factor), (supply_hbm, supply))
    own_rows = pl.ds(core * ROWS, ROWS)
    sent_rows = pl.ds((1 - core) * ROWS, ROWS)

    def load(cell, carry):
        for at, (source, target) in enumerate(arrays):
            pltpu.make_async_copy(
                source.at[sent_rows, cell], stage.at[at, cell], stage_sem.at[at]
            ).start()
            pltpu.make_async_copy(
                source.at[own_rows, cell], target.at[core * HALF + cell], own_sem.at[at]
            ).start()
        return carry

    lax.fori_loop(0, HALF, load, 0)
    pl.semaphore_wait(barrier, TILES + 2)

    own_cells = pl.ds(core * HALF, HALF)
    swaps = []
    for at, (source, target) in enumerate(arrays):
        pltpu.make_async_copy(stage.at[at], stage.at[at], stage_sem.at[at]).wait()
        copy = pltpu.make_async_remote_copy(
            src_ref=stage.at[at],
            dst_ref=target.at[own_cells],
            send_sem=swap_send.at[at],
            recv_sem=swap_recv.at[at],
            device_id=(sibling, gz),
            device_id_type=MESH,
        )
        copy.start()
        swaps.append(copy)
    for at, (source, target) in enumerate(arrays):
        pltpu.make_async_copy(
            target.at[own_cells], target.at[own_cells], own_sem.at[at]
        ).wait()
    swaps[0].wait()
    swaps[1].wait()

    lane = lax.broadcasted_iota(jnp.int32, (8, LANES), 1)
    lane_pair = lane // 2
    row_at = lax.broadcasted_iota(jnp.int32, (8, LANES), 0)

    def twice_number(tile):
        rows = (row_at + (core * ROWS + tile * 8)).astype(jnp.float32)
        ratio = 128.0 / (128.0 + rows)
        return (2.0 * diffusion_number) * (ratio * ratio)

    def scale(tile, carry):
        rows = row_block(tile)
        number = twice_number(tile)
        packed = jnp.zeros((8, LANES), jnp.float32)
        for cell in range(CELLS):
            scaled = factor[cell, rows, :] * number
            factor[cell, rows, :] = scaled
            packed = jnp.where(lane_pair == cell, pltpu.roll(scaled, 2 * cell + 1, 1), packed)
        factor_ends[rows, :] = packed
        return carry

    lax.fori_loop(0, TILES, scale, 0)

    def neighbours(source, target, slot):
        copies = []
        for side, where in enumerate((gz_down, gz_up)):
            copies.append(
                pltpu.make_async_remote_copy(
                    src_ref=source,
                    dst_ref=target.at[side],
                    send_sem=halo_send.at[slot, side],
                    recv_sem=halo_recv.at[slot, side],
                    device_id=(az, where),
                    device_id_type=MESH,
                )
            )
        return copies

    factor_copies = neighbours(factor_ends, near_factor, 0)
    for copy in factor_copies:
        copy.start()

    even = lax.rem(lane, 2) == 0
    inside = jnp.where(even, jnp.where(gz < gz_count - 1, 1.0, 0.0), jnp.where(gz > 0, 1.0, 0.0))

    def pack(tile, carry):
        rows = row_block(tile)
        packed = jnp.zeros((8, LANES), jnp.float32)
        for cell in range(CELLS):
            packed = jnp.where(
                lane_pair == cell, pltpu.roll(field[cell, rows, :], 2 * cell + 1, 1), packed
            )
        ends[rows, :] = packed
        return carry

    def explicit(step, tile):
        rows = row_block(tile)
        rate = (2.0 * lengthwise_ratio) / twice_number(tile)
        ours = ends[rows, :]
        near = jnp.where(
            even,
            pltpu.roll(near_ends[step, 0, rows, :], LANES - 1, 1),
            pltpu.roll(near_ends[step, 1, rows, :], 1, 1),
        )
        our_k = conduct(ours, factor_ends[rows, :])
        near_k = conduct(
            near,
            jnp.where(
                even,
                pltpu.roll(near_factor[0, rows, :], LANES - 1, 1),
                pltpu.roll(near_factor[1, rows, :], 1, 1),
            ),
        )
        border = rate * inside * our_k * near_k / (our_k + near_k) * (near - ours)
        last = lane == LANES - 1
        rim = jnp.logical_or(last, lane == 0)
        for cell in range(CELLS):
            here = field[cell, rows, :]
            k = conduct(here, factor[cell, rows, :])
            above = pltpu.roll(here, LANES - 1, 1)
            k_above = pltpu.roll(k, LANES - 1, 1)
            flux = rate * k * k_above / (k + k_above) * (above - here)
            flux = jnp.where(last, 0.0, flux)
            edge = jnp.where(rim, pltpu.roll(border, LANES - 1 - 2 * cell, 1), 0.0)
            total = here + (flux - pltpu.roll(flux, 1, 1) + edge) + supply[cell, rows, :]
            goal[cell, rows, :] = total
            field[cell, rows, :] = total

    def reduce_tile(tile):
        rows = row_block(tile)

        def k_of(cell):
            return conduct(field[cell, rows, :], factor[cell, rows, :])

        heads = {start: k_of(start) for start in STARTS}
        first_k = heads[0]
        state = []
        for start in STARTS:
            after = k_of(start + 1)
            link = heads[start] * after / (heads[start] + after)
            if start == 0:
                head_ground = jnp.ones((8, LANES), jnp.float32)
                head_side = goal[0, rows, :]
            else:
                head_ground = jnp.zeros((8, LANES), jnp.float32)
                head_side = jnp.zeros((8, LANES), jnp.float32)
            state.append(
                (jnp.ones((8, LANES), jnp.float32), link, goal[start + 1, rows, :], head_ground, head_side, after)
            )
        last_k = None
        for offset in range(1, 16):
            for chain, (start, end) in enumerate(zip(STARTS, ENDS)):
                cell = start + offset
                if cell >= end:
                    continue
                ground, link, side, head_ground, head_side, k = state[chain]
                after = heads[cell + 1] if cell + 1 in heads else k_of(cell + 1)
                both = k + after
                product = k * after
                inverse = 1.0 / ((ground + link) * both + product)
                own = both * inverse
                ahead = product * inverse
                back = link * own
                to_next[cell, rows, :] = ahead
                to_sep[cell, rows, :] = back
                base[cell, rows, :] = side * own
                state[chain] = (
                    1.0 + ground * ahead,
                    link * ahead,
                    goal[cell + 1, rows, :] + side * ahead,
                    head_ground + ground * back,
                    head_side + side * back,
                    after,
                )
                if cell + 1 == CELLS - 1:
                    last_k = after
        ground_16 = state[0][0] + state[1][3]
        side_16 = state[0][2] + state[1][4]
        ground_32 = state[1][0] + state[2][3]
        side_32 = state[1][2] + state[2][4]
        ground_48 = state[2][0] + state[3][3]
        side_48 = state[2][2] + state[3][4]
        ground_0, side_0 = state[0][3], state[0][4]
        ground_63, side_63 = state[3][0], state[3][2]
        links = [part[1] for part in state]

        left, right, own = eliminate(ground_16, links[0], links[1], side_16)
        to_sep[16, rows, :] = left
        to_next[16, rows, :] = right
        base[16, rows, :] = own
        ground_0 += ground_16 * left
        side_0 += side_16 * left
        ground_32 += ground_16 * right
        side_32 += side_16 * right
        link_low = links[0] * right

        left, right, own = eliminate(ground_48, links[2], links[3], side_48)
        to_sep[48, rows, :] = left
        to_next[48, rows, :] = right
        base[48, rows, :] = own
        ground_32 += ground_48 * left
        side_32 += side_48 * left
        ground_63 += ground_48 * right
        side_63 += side_48 * right
        link_high = links[2] * right

        left, right, own = eliminate(ground_32, link_low, link_high, side_32)
        to_sep[32, rows, :] = left
        to_next[32, rows, :] = right
        base[32, rows, :] = own
        ground_0 += ground_32 * left
        side_0 += side_32 * left
        ground_63 += ground_32 * right
        side_63 += side_32 * right
        link = link_low * right
        for at, value in enumerate((link, ground_0, ground_63, side_0, side_63, first_k, last_k)):
            packet[tile, at] = value

    def spread_tile(turn, tile):
        rows = row_block(tile)
        x_first = returned[turn, tile, 0]
        x_last = returned[turn, tile, 1]

        def value(cell, sep, following):
            return (
                base[cell, rows, :]
                + to_sep[cell, rows, :] * sep
                + to_next[cell, rows, :] * following
            )

        x_32 = value(32, x_first, x_last)
        x_16 = value(16, x_first, x_32)
        x_48 = value(48, x_32, x_last)
        seps = {0: x_first, 16: x_16, 32: x_32, 48: x_48, 63: x_last}
        for cell, x in seps.items():
            field[cell, rows, :] = x
        later = [seps[end] for end in ENDS]
        for offset in range(15, 0, -1):
            for chain, (start, end) in enumerate(zip(STARTS, ENDS)):
                cell = start + offset
                if cell >= end:
                    continue
                later[chain] = value(cell, seps[start], later[chain])
                field[cell, rows, :] = later[chain]

    def close_ring(turn):
        parts = [[gathered[turn, member, at] for at in range(VALUES)] for member in range(TILES)]
        count = TILES
        ground = [part[2] for part in parts]
        side = [part[4] for part in parts]
        heads = []
        links = [None] * count
        for member in range(count):
            before = (member + count - 1) % count
            link, head_ground, _, head_side, _, head_k, _ = parts[member]
            tail_k = parts[before][6]
            both = tail_k + head_k
            product = tail_k * head_k
            inverse = 1.0 / ((head_ground + link) * both + product)
            own = both * inverse
            to_before = product * inverse
            to_last = link * own
            heads.append((to_before, to_last, head_side * own))
            links[member] = link * to_before
            ground[before] = ground[before] + head_ground * to_before
            side[before] = side[before] + head_side * to_before
            ground[member] = ground[member] + head_ground * to_last
            side[member] = side[member] + head_side * to_last
        undo = []
        nodes = list(range(count))
        while len(nodes) > 2:
            size = len(nodes)
            kept_links = []
            for at in range(1, size, 2):
                node, low, high = nodes[at], nodes[at - 1], nodes[(at + 1) % size]
                to_low, to_high, own = eliminate(ground[node], links[at], links[(at + 1) % size], side[node])
                undo.append((node, low, high, to_low, to_high, own))
                ground[low] = ground[low] + ground[node] * to_low
                side[low] = side[low] + side[node] * to_low
                ground[high] = ground[high] + ground[node] * to_high
                side[high] = side[high] + side[node] * to_high
                kept_links.append(links[at] * to_high)
            nodes = nodes[::2]
            links = kept_links[-1:] + kept_links[:-1]
        low, high = nodes
        link = links[0] + links[1]
        inverse = 1.0 / (ground[high] + link)
        to_low = link * inverse
        x = [None] * count
        x[low] = (side[low] + side[high] * to_low) / (ground[low] + ground[high] * to_low)
        x[high] = side[high] * inverse + to_low * x[low]
        for node, low, high, to_low, to_high, own in reversed(undo):
            x[node] = own + to_low * x[low] + to_high * x[high]
        for member in range(count):
            to_before, to_last, own = heads[member]
            answer[turn, member, 0] = own + to_before * x[(member + count - 1) % count] + to_last * x[member]
            answer[turn, member, 1] = x[member]

    y_at = lax.rem(chip, 4)

    def ordered(at):
        pair = at // 2
        shift = jnp.where(pair == 0, 2, jnp.where(pair == 3, 0, 2 * pair - 1))
        return lax.rem(y_at + shift, 4) + 4 * lax.rem(at, 2)

    def packet_copy(turn, tile):
        return pltpu.make_async_remote_copy(
            src_ref=packet.at[tile],
            dst_ref=gathered.at[turn, chip],
            send_sem=packet_send.at[turn],
            recv_sem=packet_recv.at[turn],
            device_id=(2 * tile + core, across),
            device_id_type=MESH,
        )

    def answer_copy(turn, member):
        return pltpu.make_async_remote_copy(
            src_ref=answer.at[turn, member],
            dst_ref=returned.at[turn, chip],
            send_sem=answer_send.at[turn],
            recv_sem=answer_recv.at[turn, chip],
            device_id=(2 * member + core, across),
            device_id_type=MESH,
        )

    def time_step(step, carry):
        lax.fori_loop(0, TILES, pack, 0)
        copies = neighbours(ends, near_ends.at[step], 1 + step)
        for copy in copies:
            copy.start()

        @pl.when(step == 0)
        def _():
            for copy in factor_copies:
                copy.wait()
            swaps[2].wait()

        for copy in copies:
            copy.wait()

        def explicit_tile(tile, inner):
            explicit(step, tile)
            return inner

        lax.fori_loop(0, TILES, explicit_tile, 0)

        def sweep(picard, inner):
            turn = PICARD * step + picard

            def forward(at, state):
                tile = ordered(at)
                reduce_tile(tile)
                packet_copy(turn, tile).start()
                return state

            lax.fori_loop(0, TILES, forward, 0)
            pltpu.make_async_copy(
                gathered.at[turn], gathered.at[turn], packet_recv.at[turn]
            ).wait()
            close_ring(turn)

            def reply(at, state):
                answer_copy(turn, ordered(at)).start()
                return state

            lax.fori_loop(0, TILES, reply, 0)

            def backward(at, state):
                tile = ordered(TILES - 1 - at)
                pltpu.make_async_copy(
                    returned.at[turn, tile], returned.at[turn, tile], answer_recv.at[turn, tile]
                ).wait()
                spread_tile(turn, tile)
                return state

            lax.fori_loop(0, TILES, backward, 0)
            pltpu.make_async_copy(packet, packet, packet_send.at[turn]).wait()
            pltpu.make_async_copy(
                answer.at[turn], answer.at[turn], answer_send.at[turn]
            ).wait()
            return inner

        lax.fori_loop(0, PICARD, sweep, 0)
        return carry

    lax.fori_loop(0, STEPS, time_step, 0)

    def remote_out(cell):
        return pltpu.make_async_remote_copy(
            src_ref=field.at[(1 - core) * HALF + cell],
            dst_ref=out_hbm.at[own_rows, cell],
            send_sem=out_send,
            recv_sem=out_recv,
            device_id=(sibling, gz),
            device_id_type=MESH,
        )

    def unload(cell, carry):
        remote_out(cell).start()
        pltpu.make_async_copy(
            field.at[core * HALF + cell], out_hbm.at[own_rows, cell], out_sem
        ).start()
        return carry

    lax.fori_loop(0, HALF, unload, 0)
    whole = field.at[pl.ds(0, HALF)]
    pltpu.make_async_copy(whole, whole, out_sem).wait()
    pltpu.make_async_copy(whole, whole, out_send).wait()
    pltpu.make_async_copy(whole, whole, out_recv).wait()


def shards(starting_warmth, volume_transfer_multiplier, energy_supply_history):
    cells = pltpu.VMEM((CELLS, ROWS, LANES), jnp.float32)
    dma = pltpu.SemaphoreType.DMA
    turns = STEPS * PICARD
    anywhere = pl.BlockSpec(memory_space=pltpu.HBM)
    return pl.pallas_call(
        kernel,
        out_shape=jax.ShapeDtypeStruct(starting_warmth.shape, jnp.float32),
        in_specs=[anywhere] * 3,
        out_specs=anywhere,
        scratch_shapes=[
            cells, cells, cells, cells, cells, cells, cells,
            pltpu.VMEM((3, HALF, ROWS, LANES), jnp.float32),
            pltpu.VMEM((ROWS, LANES), jnp.float32),
            pltpu.VMEM((ROWS, LANES), jnp.float32),
            pltpu.VMEM((STEPS, 2, ROWS, LANES), jnp.float32),
            pltpu.VMEM((2, ROWS, LANES), jnp.float32),
            pltpu.VMEM((TILES, VALUES, 8, LANES), jnp.float32),
            pltpu.VMEM((turns, TILES, VALUES, 8, LANES), jnp.float32),
            pltpu.VMEM((turns, TILES, 2, 8, LANES), jnp.float32),
            pltpu.VMEM((turns, TILES, 2, 8, LANES), jnp.float32),
            dma((3,)), dma((3,)), dma((3,)), dma((3,)),
            dma((1 + STEPS, 2)), dma((1 + STEPS, 2)),
            dma((turns,)), dma((turns,)), dma((turns,)), dma((turns, TILES)),
            dma, dma, dma,
        ],
        compiler_params=pltpu.CompilerParams(
            collective_id=0, has_side_effects=True, vmem_limit_bytes=40 * 1024 * 1024
        ),
        name="annulus",
    )(starting_warmth, volume_transfer_multiplier, energy_supply_history)


def solution(mesh):
    placed = (P(None, "az", "gz"), P(None, "az", "gz"), P(None, "az", "gz"))
    return jax.shard_map(
        shards, mesh=mesh, in_specs=placed, out_specs=P(None, "az", "gz"), check_vma=False
    )
```

```python
import functools
import types

import jax
import jax.numpy as jnp
from jax import lax
from jax.experimental import pallas as pl
from jax.experimental.pallas import tpu as pltpu
from jax.sharding import PartitionSpec as P

STEPS = 2
PICARD = 2
diffusion_number = 1000.0
lengthwise_ratio = 0.048

MESH = pl.DeviceIdType.MESH
CELLS = 64
HALF = 32
ROWS = 64
TILES = 8
PART = 4
LANES = 128
VALUES = 7
GROUP = 16
STARTS = (0, 16, 32, 48)
ENDS = (16, 32, 48, 63)


def row_block(tile):
    return pl.ds(pl.multiple_of(tile * 8, 8), 8)


def conduct(field, factor):
    return factor * (1.5 + jnp.tanh(field))


def eliminate(ground, left, right, side):
    inverse = 1.0 / (ground + left + right)
    to_left = left * inverse
    to_right = right * inverse
    return to_left, to_right, side * inverse


def lane_at():
    return lax.broadcasted_iota(jnp.int32, (8, LANES), 1)


def twice_number(core, tile):
    rows = (lax.broadcasted_iota(jnp.int32, (8, LANES), 0) + (core * ROWS + tile * 8)).astype(jnp.float32)
    ratio = 128.0 / (128.0 + rows)
    return (2.0 * diffusion_number) * (ratio * ratio)


def first_rows(tile):
    rows = (lax.broadcasted_iota(jnp.int32, (8, LANES), 0) + tile * 8).astype(jnp.float32)
    ratio = 128.0 / (128.0 + rows)
    return (2.0 * diffusion_number) * (ratio * ratio)


def prepare(r, core, tile):
    rows = row_block(tile)
    lane_pair = lane_at() // 2
    number = first_rows(tile)
    packed = jnp.zeros((8, LANES), jnp.float32)
    packed_factor = jnp.zeros((8, LANES), jnp.float32)
    for cell in range(HALF):
        here = lane_pair == cell
        scaled = r.own_factor[cell, rows, :] * number
        r.scaled[cell, rows, :] = scaled
        packed = jnp.where(here, pltpu.roll(r.own_field[cell, rows, :], 2 * cell + 1, 1), packed)
        packed_factor = jnp.where(here, pltpu.roll(scaled, 2 * cell + 1, 1), packed_factor)
    r.own_ends[0, rows, :] = jnp.where(core == 0, packed, pltpu.roll(packed, 64, 1))
    r.own_ends[1, rows, :] = jnp.where(core == 0, packed_factor, pltpu.roll(packed_factor, 64, 1))


def merge(r, core, tile):
    rows = row_block(tile)
    low = lane_at() < 64
    ours = jnp.where(core == 0, jnp.where(low, 1, 0), jnp.where(low, 0, 1)) == 1
    held = pl.ds(pl.multiple_of(core * ROWS + tile * 8, 8), 8)
    r.ends[0, rows, :] = jnp.where(ours, r.own_ends[0, held, :], r.paired_ends[0, rows, :])
    r.factor_ends[rows, :] = jnp.where(ours, r.own_ends[1, held, :], r.paired_ends[1, rows, :])
    for side in range(2):
        r.near_ends[0, side, rows, :] = jnp.where(
            low, r.halves[side, 0, 0, rows, :], r.halves[side, 1, 0, rows, :]
        )
        r.near_factor[side, rows, :] = jnp.where(
            low, r.halves[side, 0, 1, rows, :], r.halves[side, 1, 1, rows, :]
        )


def border_of(r, core, low_gz, high_gz, step, tile):
    rows = row_block(tile)
    rate = (2.0 * lengthwise_ratio) / twice_number(core, tile)
    even = lax.rem(lane_at(), 2) == 0
    inside = jnp.where(even, high_gz, low_gz)
    ours = r.ends[step, rows, :]
    near = jnp.where(
        even,
        pltpu.roll(r.near_ends[step, 0, rows, :], LANES - 1, 1),
        pltpu.roll(r.near_ends[step, 1, rows, :], 1, 1),
    )
    near_factor = jnp.where(
        even,
        pltpu.roll(r.near_factor[0, rows, :], LANES - 1, 1),
        pltpu.roll(r.near_factor[1, rows, :], 1, 1),
    )
    our_k = conduct(ours, r.factor_ends[rows, :])
    near_k = conduct(near, near_factor)
    return rate * inside * our_k * near_k / (our_k + near_k) * (near - ours)


def explicit(number, field, factor, beyond, supply, rows, cells, store):
    rate = (2.0 * lengthwise_ratio) / number
    last = lane_at() == LANES - 1
    for group in range(0, cells, GROUP):
        at = range(group, group + GROUP)
        here = [field[cell, rows, :] for cell in at]
        k = [conduct(x, factor[cell, rows, :]) for cell, x in zip(at, here)]
        above = [pltpu.roll(x, LANES - 1, 1) for x in here]
        if beyond is None:
            k_above = [pltpu.roll(x, LANES - 1, 1) for x in k]
        else:
            k_above = [conduct(x, beyond[cell, rows, :]) for cell, x in zip(at, above)]
        flux = [
            jnp.where(last, 0.0, rate * k[i] * k_above[i] / (k[i] + k_above[i]) * (above[i] - here[i]))
            for i in range(GROUP)
        ]
        below = [pltpu.roll(x, 1, 1) for x in flux]
        for i, cell in enumerate(at):
            store(cell, here[i] + (flux[i] - below[i]) + supply[cell, rows, :])


def explicit_first(r, target, base, row_shift, tile):
    rows = row_block(tile)
    placed = pl.ds(pl.multiple_of(tile * 8 - row_shift, 8), 8)

    def store(cell, value):
        target[base + cell, placed, :] = value

    explicit(first_rows(tile), r.own_field, r.scaled, None, r.own_supply, rows, HALF, store)


def explicit_later(r, core, tile):
    rows = row_block(tile)

    def store(cell, value):
        r.raw[cell, rows, :] = value

    explicit(
        twice_number(core, tile), r.field, r.factor, r.beyond, r.supply, rows, CELLS, store
    )


def shift_factor(r, tile):
    rows = row_block(tile)
    for cell in range(CELLS):
        r.beyond[cell, rows, :] = pltpu.roll(r.factor[cell, rows, :], LANES - 1, 1)


def reduce_tile(r, border, tile):
    rows = row_block(tile)
    lane = lane_at()
    rim = jnp.logical_or(lane == 0, lane == LANES - 1)

    def k_of(cell):
        if border is None:
            return conduct(r.field[cell, rows, :], r.factor[cell, rows, :]), r.goal[cell, rows, :]
        edge = jnp.where(rim, pltpu.roll(border, LANES - 1 - 2 * cell, 1), 0.0)
        total = r.raw[cell, rows, :] + edge
        r.goal[cell, rows, :] = total
        return conduct(total, r.factor[cell, rows, :]), total

    heads = {start: k_of(start) for start in STARTS}
    first_k = heads[0][0]
    state = []
    for start in STARTS:
        after, after_side = k_of(start + 1)
        head_k = heads[start][0]
        link = head_k * after / (head_k + after)
        if start == 0:
            head_ground = jnp.ones((8, LANES), jnp.float32)
            head_side = heads[0][1]
        else:
            head_ground = jnp.zeros((8, LANES), jnp.float32)
            head_side = jnp.zeros((8, LANES), jnp.float32)
        state.append(
            (jnp.ones((8, LANES), jnp.float32), link, after_side, head_ground, head_side, after)
        )
    last_k = None
    for offset in range(1, 16):
        for chain, (start, end) in enumerate(zip(STARTS, ENDS)):
            cell = start + offset
            if cell >= end:
                continue
            ground, link, side, head_ground, head_side, k = state[chain]
            after, after_side = heads[cell + 1] if cell + 1 in heads else k_of(cell + 1)
            both = k + after
            product = k * after
            inverse = 1.0 / ((ground + link) * both + product)
            own = both * inverse
            ahead = product * inverse
            back = link * own
            r.to_next[cell, rows, :] = ahead
            r.to_sep[cell, rows, :] = back
            r.base[cell, rows, :] = side * own
            state[chain] = (
                1.0 + ground * ahead,
                link * ahead,
                after_side + side * ahead,
                head_ground + ground * back,
                head_side + side * back,
                after,
            )
            if cell + 1 == CELLS - 1:
                last_k = after
    ground_16 = state[0][0] + state[1][3]
    side_16 = state[0][2] + state[1][4]
    ground_32 = state[1][0] + state[2][3]
    side_32 = state[1][2] + state[2][4]
    ground_48 = state[2][0] + state[3][3]
    side_48 = state[2][2] + state[3][4]
    ground_0, side_0 = state[0][3], state[0][4]
    ground_63, side_63 = state[3][0], state[3][2]
    links = [part[1] for part in state]

    left, right, own = eliminate(ground_16, links[0], links[1], side_16)
    r.to_sep[16, rows, :] = left
    r.to_next[16, rows, :] = right
    r.base[16, rows, :] = own
    ground_0 += ground_16 * left
    side_0 += side_16 * left
    ground_32 += ground_16 * right
    side_32 += side_16 * right
    link_low = links[0] * right

    left, right, own = eliminate(ground_48, links[2], links[3], side_48)
    r.to_sep[48, rows, :] = left
    r.to_next[48, rows, :] = right
    r.base[48, rows, :] = own
    ground_32 += ground_48 * left
    side_32 += side_48 * left
    ground_63 += ground_48 * right
    side_63 += side_48 * right
    link_high = links[2] * right

    left, right, own = eliminate(ground_32, link_low, link_high, side_32)
    r.to_sep[32, rows, :] = left
    r.to_next[32, rows, :] = right
    r.base[32, rows, :] = own
    ground_0 += ground_32 * left
    side_0 += side_32 * left
    ground_63 += ground_32 * right
    side_63 += side_32 * right
    link = link_low * right
    for at, value in enumerate((link, ground_0, ground_63, side_0, side_63, first_k, last_k)):
        r.packet[tile, at] = value


def spread_tile(r, turn, pack_to, tile):
    rows = row_block(tile)
    x_first = r.returned[turn, tile, 0]
    x_last = r.returned[turn, tile, 1]
    lane_pair = lane_at() // 2
    packed = [jnp.zeros((8, LANES), jnp.float32)]

    def value(cell, sep, following):
        return (
            r.base[cell, rows, :]
            + r.to_sep[cell, rows, :] * sep
            + r.to_next[cell, rows, :] * following
        )

    def keep(cell, x):
        r.field[cell, rows, :] = x
        if pack_to is not None:
            packed[0] = jnp.where(lane_pair == cell, pltpu.roll(x, 2 * cell + 1, 1), packed[0])

    x_32 = value(32, x_first, x_last)
    x_16 = value(16, x_first, x_32)
    x_48 = value(48, x_32, x_last)
    seps = {0: x_first, 16: x_16, 32: x_32, 48: x_48, 63: x_last}
    for cell, x in seps.items():
        keep(cell, x)
    later = [seps[end] for end in ENDS]
    for offset in range(15, 0, -1):
        for chain, (start, end) in enumerate(zip(STARTS, ENDS)):
            cell = start + offset
            if cell >= end:
                continue
            later[chain] = value(cell, seps[start], later[chain])
            keep(cell, later[chain])
    if pack_to is not None:
        r.ends[pack_to, rows, :] = packed[0]


def close_ring(r, turn):
    parts = [[r.gathered[turn, member, at] for at in range(VALUES)] for member in range(TILES)]
    count = TILES
    ground = [part[2] for part in parts]
    side = [part[4] for part in parts]
    heads = []
    links = [None] * count
    for member in range(count):
        before = (member + count - 1) % count
        link, head_ground, _, head_side, _, head_k, _ = parts[member]
        tail_k = parts[before][6]
        both = tail_k + head_k
        product = tail_k * head_k
        inverse = 1.0 / ((head_ground + link) * both + product)
        own = both * inverse
        to_before = product * inverse
        to_last = link * own
        heads.append((to_before, to_last, head_side * own))
        links[member] = link * to_before
        ground[before] = ground[before] + head_ground * to_before
        side[before] = side[before] + head_side * to_before
        ground[member] = ground[member] + head_ground * to_last
        side[member] = side[member] + head_side * to_last
    undo = []
    nodes = list(range(count))
    while len(nodes) > 2:
        size = len(nodes)
        kept_links = []
        for at in range(1, size, 2):
            node, low, high = nodes[at], nodes[at - 1], nodes[(at + 1) % size]
            to_low, to_high, own = eliminate(ground[node], links[at], links[(at + 1) % size], side[node])
            undo.append((node, low, high, to_low, to_high, own))
            ground[low] = ground[low] + ground[node] * to_low
            side[low] = side[low] + side[node] * to_low
            ground[high] = ground[high] + ground[node] * to_high
            side[high] = side[high] + side[node] * to_high
            kept_links.append(links[at] * to_high)
        nodes = nodes[::2]
        links = kept_links[-1:] + kept_links[:-1]
    low, high = nodes
    link = links[0] + links[1]
    inverse = 1.0 / (ground[high] + link)
    to_low = link * inverse
    x = [None] * count
    x[low] = (side[low] + side[high] * to_low) / (ground[low] + ground[high] * to_low)
    x[high] = side[high] * inverse + to_low * x[low]
    for node, low, high, to_low, to_high, own in reversed(undo):
        x[node] = own + to_low * x[low] + to_high * x[high]
    for member in range(count):
        to_before, to_last, own = heads[member]
        r.answer[turn, member, 0] = own + to_before * x[(member + count - 1) % count] + to_last * x[member]
        r.answer[turn, member, 1] = x[member]


NAMES = (
    "field", "factor", "beyond", "supply", "raw", "goal", "to_sep", "to_next", "base",
    "own_field", "own_factor", "own_supply", "scaled", "stage",
    "own_ends", "paired_ends", "halves", "ends", "factor_ends", "near_ends", "near_factor",
    "packet", "gathered", "answer", "returned",
    "load_sem", "move_sem", "swap_send", "swap_recv", "first_send", "first_recv",
    "halo_send", "halo_recv", "packet_send", "packet_recv", "answer_send", "answer_recv",
    "out_sem", "out_send", "out_recv",
)


def kernel(warmth_hbm, factor_hbm, supply_hbm, out_hbm, *refs):
    r = types.SimpleNamespace(**dict(zip(NAMES, refs)))
    az = lax.axis_index("az")
    gz = lax.axis_index("gz")
    core = lax.rem(az, 2)
    chip = az // 2
    sibling = az + 1 - 2 * core
    gz_count = lax.axis_size("gz")
    across = gz + 1 - 2 * lax.rem(gz, 2)
    gz_up = lax.rem(gz + 1, gz_count)
    gz_down = lax.rem(gz + gz_count - 1, gz_count)
    other = lax.rem(gz + gz_count - 1 + 2 * lax.rem(gz, 2), gz_count)
    low_gz = jnp.where(gz > 0, 1.0, 0.0)
    high_gz = jnp.where(gz < gz_count - 1, 1.0, 0.0)

    barrier = pltpu.get_barrier_semaphore()
    for member in range(TILES):
        pl.semaphore_signal(
            barrier, inc=1, device_id=(2 * member + core, across), device_id_type=MESH
        )
    for where in ((sibling, gz), (az, other), (sibling, across), (sibling, other)):
        pl.semaphore_signal(barrier, inc=1, device_id=where, device_id_type=MESH)

    def for_range(low, high, work):
        def one(at, carry):
            work(at)
            return carry

        lax.fori_loop(low, high, one, 0)

    def remote(source, target, send_sem, recv_sem, where):
        return pltpu.make_async_remote_copy(
            src_ref=source, dst_ref=target, send_sem=send_sem, recv_sem=recv_sem,
            device_id=where, device_id_type=MESH,
        )

    def wait_for(ref, sem):
        pltpu.make_async_copy(ref, ref, sem).wait()

    loads = ((warmth_hbm, r.own_field), (factor_hbm, r.own_factor), (supply_hbm, r.own_supply))

    def load(cell):
        for at, (source, target) in enumerate(loads):
            pltpu.make_async_copy(source.at[:, cell], target.at[cell], r.load_sem.at[at]).start()

    for_range(0, HALF, load)
    for at in range(2):
        wait_for(loads[at][1], r.load_sem.at[at])

    own_rows = pl.ds(core * ROWS, ROWS)
    sent_rows = pl.ds((1 - core) * ROWS, ROWS)
    own_cells = pl.ds(core * HALF, HALF)
    sent_tile = (1 - core) * TILES
    own_tile = core * TILES

    for_range(sent_tile, sent_tile + TILES, functools.partial(prepare, r, core))
    pl.semaphore_wait(barrier, TILES + 4)
    factor_swap = remote(
        r.scaled.at[:, sent_rows], r.factor.at[own_cells],
        r.swap_send.at[0], r.swap_recv.at[0], (sibling, gz),
    )
    factor_swap.start()
    for_range(own_tile, own_tile + TILES, functools.partial(prepare, r, core))
    factor_move = pltpu.make_async_copy(
        r.scaled.at[:, own_rows], r.factor.at[own_cells], r.move_sem.at[0]
    )
    factor_move.start()
    firsts = []
    for side, where in enumerate((gz_down, gz_up)):
        for same in range(2):
            firsts.append(
                remote(
                    r.own_ends.at[:, own_rows if same else sent_rows],
                    r.halves.at[side, core],
                    r.first_send.at[2 * side + same],
                    r.first_recv.at[2 * side + core],
                    (az if same else sibling, where),
                )
            )
    firsts.append(
        remote(
            r.own_ends.at[:, sent_rows], r.paired_ends,
            r.first_send.at[4], r.first_recv.at[4], (sibling, gz),
        )
    )
    for copy in firsts:
        copy.start()
    wait_for(r.own_supply, r.load_sem.at[2])

    goal_swaps = []
    for chunk in range(2):
        low = sent_tile + PART * chunk
        for_range(
            low, low + PART,
            functools.partial(explicit_first, r, r.stage, 0, sent_tile * 8),
        )
        rows = pl.ds(PART * 8 * chunk, PART * 8)
        goal_swaps.append(
            remote(
                r.stage.at[:, rows], r.raw.at[own_cells, rows],
                r.swap_send.at[1 + chunk], r.swap_recv.at[1 + chunk], (sibling, gz),
            )
        )
        goal_swaps[-1].start()
    supply_swap = remote(
        r.own_supply.at[:, sent_rows], r.supply.at[own_cells],
        r.swap_send.at[3], r.swap_recv.at[3], (sibling, gz),
    )
    supply_swap.start()
    supply_move = pltpu.make_async_copy(
        r.own_supply.at[:, own_rows], r.supply.at[own_cells], r.move_sem.at[1]
    )
    supply_move.start()
    for_range(
        own_tile, own_tile + TILES,
        functools.partial(explicit_first, r, r.raw, core * HALF, own_tile * 8),
    )
    for side in range(2):
        for source in range(2):
            wait_for(r.halves.at[side, source], r.first_recv.at[2 * side + source])
    wait_for(r.paired_ends, r.first_recv.at[4])
    for_range(0, TILES, functools.partial(merge, r, core))
    factor_move.wait()
    factor_swap.wait_recv()

    y_at = lax.rem(chip, 4)

    def ordered(chunk, at):
        shift = jnp.where(at == 0, 2, jnp.where(at == 3, 0, 2 * at - 1))
        return PART * chunk + lax.rem(y_at + shift, 4)

    def forward(step, picard, chunk):
        turn = PICARD * step + picard

        def work(at):
            tile = ordered(chunk, at)
            border = None if picard else border_of(r, core, low_gz, high_gz, step, tile)
            reduce_tile(r, border, tile)
            remote(
                r.packet.at[tile], r.gathered.at[turn, chip],
                r.packet_send.at[turn], r.packet_recv.at[turn], (2 * tile + core, across),
            ).start()

        for_range(0, PART, work)

    def solve(turn):
        wait_for(r.gathered.at[turn], r.packet_recv.at[turn])
        close_ring(r, turn)

        def reply(at):
            member = ordered(lax.rem(at, 2), at // 2)
            remote(
                r.answer.at[turn, member], r.returned.at[turn, chip],
                r.answer_send.at[turn], r.answer_recv.at[turn, chip],
                (2 * member + core, across),
            ).start()

        for_range(0, TILES, reply)
        wait_for(r.packet, r.packet_send.at[turn])

    def backward(turn, chunk, pack_to):
        def work(at):
            tile = ordered(chunk, PART - 1 - at)
            wait_for(r.returned.at[turn, tile], r.answer_recv.at[turn, tile])
            spread_tile(r, turn, pack_to, tile)

        for_range(0, PART, work)

    halos = [[], []]
    for step in range(STEPS):
        for chunk in range(2):
            rows = pl.ds(PART * 8 * chunk, PART * 8)
            if step == 0:
                goal_swaps[chunk].wait_recv()
            else:
                low = PART * chunk
                for_range(low, low + PART, functools.partial(explicit_later, r, core))
                for copy in halos[chunk]:
                    copy.wait()
            forward(step, 0, chunk)
        if step == 0:
            for_range(0, TILES, functools.partial(shift_factor, r))
        for picard in range(PICARD):
            turn = PICARD * step + picard
            final = picard == PICARD - 1
            solve(turn)
            for chunk in range(2):
                last = step == STEPS - 1
                backward(turn, chunk, step + 1 if final and not last else None)
                if not final:
                    forward(step, picard + 1, chunk)
                elif not last:
                    rows = pl.ds(PART * 8 * chunk, PART * 8)
                    for side, where in enumerate((gz_down, gz_up)):
                        copy = remote(
                            r.ends.at[step + 1, rows], r.near_ends.at[step + 1, side, rows],
                            r.halo_send.at[chunk, side], r.halo_recv.at[chunk, side],
                            (az, where),
                        )
                        copy.start()
                        halos[chunk].append(copy)
            wait_for(r.answer.at[turn], r.answer_send.at[turn])
        if step == 0:
            supply_swap.wait_recv()
            supply_move.wait()

    def unload(cell):
        remote(
            r.field.at[(1 - core) * HALF + cell], out_hbm.at[own_rows, cell],
            r.out_send, r.out_recv, (sibling, gz),
        ).start()
        pltpu.make_async_copy(
            r.field.at[core * HALF + cell], out_hbm.at[own_rows, cell], r.out_sem
        ).start()

    for_range(0, HALF, unload)
    for copy in [factor_swap, supply_swap] + goal_swaps + firsts:
        copy.wait_send()
    whole = r.field.at[pl.ds(0, HALF)]
    wait_for(whole, r.out_sem)
    wait_for(whole, r.out_send)
    wait_for(whole, r.out_recv)


def shards(starting_warmth, volume_transfer_multiplier, energy_supply_history):
    def real(*shape):
        return pltpu.VMEM(shape + (LANES,), jnp.float32)

    cells = real(CELLS, ROWS)
    own = real(HALF, 2 * ROWS)
    dma = pltpu.SemaphoreType.DMA
    turns = STEPS * PICARD
    anywhere = pl.BlockSpec(memory_space=pltpu.HBM)
    return pl.pallas_call(
        kernel,
        out_shape=jax.ShapeDtypeStruct(starting_warmth.shape, jnp.float32),
        in_specs=[anywhere] * 3,
        out_specs=anywhere,
        scratch_shapes=[cells] * 9 + [own] * 4 + [
            real(HALF, ROWS),
            real(2, 2 * ROWS), real(2, ROWS), real(2, 2, 2, ROWS), real(STEPS, ROWS),
            real(ROWS), real(STEPS, 2, ROWS), real(2, ROWS),
            real(TILES, VALUES, 8), real(turns, TILES, VALUES, 8),
            real(turns, TILES, 2, 8), real(turns, TILES, 2, 8),
            dma((3,)), dma((2,)), dma((4,)), dma((4,)), dma((5,)), dma((5,)),
            dma((2, 2)), dma((2, 2)),
            dma((turns,)), dma((turns,)), dma((turns,)), dma((turns, TILES)),
            dma, dma, dma,
        ],
        compiler_params=pltpu.CompilerParams(
            collective_id=0, has_side_effects=True, vmem_limit_bytes=60 * 1024 * 1024
        ),
        name="annulus",
    )(starting_warmth, volume_transfer_multiplier, energy_supply_history)


def solution(mesh):
    placed = (P(None, "az", "gz"), P(None, "az", "gz"), P(None, "az", "gz"))
    return jax.shard_map(
        shards, mesh=mesh, in_specs=placed, out_specs=P(None, "az", "gz"), check_vma=False
    )
```

```python
import functools
import types

import jax
import jax.numpy as jnp
from jax import lax
from jax.experimental import pallas as pl
from jax.experimental.pallas import tpu as pltpu
from jax.sharding import PartitionSpec as P

STEPS = 2
PICARD = 2
diffusion_number = 1000.0
lengthwise_ratio = 0.048

MESH = pl.DeviceIdType.MESH
CELLS = 64
HALF = 32
ROWS = 64
TILES = 8
PART = 4
LANES = 128
VALUES = 5
GROUP = 16
STARTS = (0, 16, 32, 48)
ENDS = (16, 32, 48, 63)


def row_block(tile):
    return pl.ds(pl.multiple_of(tile * 8, 8), 8)


def conduct(field, factor):
    return factor * (1.5 + jnp.tanh(field))


def eliminate(ground, left, right, side):
    inverse = 1.0 / (ground + left + right)
    to_left = left * inverse
    to_right = right * inverse
    return to_left, to_right, side * inverse


def lane_at():
    return lax.broadcasted_iota(jnp.int32, (8, LANES), 1)


def twice_number(core, tile):
    rows = (lax.broadcasted_iota(jnp.int32, (8, LANES), 0) + (core * ROWS + tile * 8)).astype(jnp.float32)
    ratio = 128.0 / (128.0 + rows)
    return (2.0 * diffusion_number) * (ratio * ratio)


def first_rows(tile):
    rows = (lax.broadcasted_iota(jnp.int32, (8, LANES), 0) + tile * 8).astype(jnp.float32)
    ratio = 128.0 / (128.0 + rows)
    return (2.0 * diffusion_number) * (ratio * ratio)


def prepare(r, core, tile):
    rows = row_block(tile)
    lane_pair = lane_at() // 2
    number = first_rows(tile)
    packed = jnp.zeros((8, LANES), jnp.float32)
    packed_factor = jnp.zeros((8, LANES), jnp.float32)
    for cell in range(HALF):
        here = lane_pair == cell
        scaled = r.own_factor[cell, rows, :] * number
        r.scaled[cell, rows, :] = scaled
        packed = jnp.where(here, pltpu.roll(r.own_field[cell, rows, :], 2 * cell + 1, 1), packed)
        packed_factor = jnp.where(here, pltpu.roll(scaled, 2 * cell + 1, 1), packed_factor)
    r.own_ends[0, rows, :] = jnp.where(core == 0, packed, pltpu.roll(packed, 64, 1))
    r.own_ends[1, rows, :] = jnp.where(core == 0, packed_factor, pltpu.roll(packed_factor, 64, 1))


def merge(r, core, tile):
    rows = row_block(tile)
    low = lane_at() < 64
    ours = jnp.where(core == 0, jnp.where(low, 1, 0), jnp.where(low, 0, 1)) == 1
    held = pl.ds(pl.multiple_of(core * ROWS + tile * 8, 8), 8)
    r.ends[0, rows, :] = jnp.where(ours, r.own_ends[0, held, :], r.paired_ends[0, rows, :])
    r.factor_ends[rows, :] = jnp.where(ours, r.own_ends[1, held, :], r.paired_ends[1, rows, :])
    for side in range(2):
        r.near_ends[0, side, rows, :] = jnp.where(
            low, r.halves[side, 0, 0, rows, :], r.halves[side, 1, 0, rows, :]
        )
        r.near_factor[side, rows, :] = jnp.where(
            low, r.halves[side, 0, 1, rows, :], r.halves[side, 1, 1, rows, :]
        )


def border_of(r, core, low_gz, high_gz, step, tile):
    rows = row_block(tile)
    rate = (2.0 * lengthwise_ratio) / twice_number(core, tile)
    even = lax.rem(lane_at(), 2) == 0
    inside = jnp.where(even, high_gz, low_gz)
    ours = r.ends[step, rows, :]
    near = jnp.where(
        even,
        pltpu.roll(r.near_ends[step, 0, rows, :], LANES - 1, 1),
        pltpu.roll(r.near_ends[step, 1, rows, :], 1, 1),
    )
    near_factor = jnp.where(
        even,
        pltpu.roll(r.near_factor[0, rows, :], LANES - 1, 1),
        pltpu.roll(r.near_factor[1, rows, :], 1, 1),
    )
    our_k = conduct(ours, r.factor_ends[rows, :])
    near_k = conduct(near, near_factor)
    return rate * inside * our_k * near_k / (our_k + near_k) * (near - ours)


def explicit(number, field, factor, beyond, supply, rows, cells, store):
    rate = (2.0 * lengthwise_ratio) / number
    last = lane_at() == LANES - 1
    for group in range(0, cells, GROUP):
        at = range(group, group + GROUP)
        here = [field[cell, rows, :] for cell in at]
        k = [conduct(x, factor[cell, rows, :]) for cell, x in zip(at, here)]
        above = [pltpu.roll(x, LANES - 1, 1) for x in here]
        if beyond is None:
            k_above = [pltpu.roll(x, LANES - 1, 1) for x in k]
        else:
            k_above = [conduct(x, beyond[cell, rows, :]) for cell, x in zip(at, above)]
        flux = [
            jnp.where(last, 0.0, rate * k[i] * k_above[i] / (k[i] + k_above[i]) * (above[i] - here[i]))
            for i in range(GROUP)
        ]
        below = [pltpu.roll(x, 1, 1) for x in flux]
        for i, cell in enumerate(at):
            store(cell, here[i] + (flux[i] - below[i]) + supply[cell, rows, :])


def explicit_first(r, target, base, row_shift, tile):
    rows = row_block(tile)
    placed = pl.ds(pl.multiple_of(tile * 8 - row_shift, 8), 8)

    def store(cell, value):
        target[base + cell, placed, :] = value

    explicit(first_rows(tile), r.own_field, r.scaled, None, r.own_supply, rows, HALF, store)


def explicit_later(r, core, tile):
    rows = row_block(tile)

    def store(cell, value):
        r.raw[cell, rows, :] = value

    explicit(
        twice_number(core, tile), r.field, r.factor, r.beyond, r.supply, rows, CELLS, store
    )


def shift_factor(r, tile):
    rows = row_block(tile)
    for cell in range(CELLS):
        r.beyond[cell, rows, :] = pltpu.roll(r.factor[cell, rows, :], LANES - 1, 1)


def reduce_tile(r, border, turn, tile):
    rows = row_block(tile)
    lane = lane_at()
    rim = jnp.logical_or(lane == 0, lane == LANES - 1)

    def k_of(cell):
        if border is None:
            return conduct(r.field[cell, rows, :], r.factor[cell, rows, :]), r.goal[cell, rows, :]
        edge = jnp.where(rim, pltpu.roll(border, LANES - 1 - 2 * cell, 1), 0.0)
        total = r.raw[cell, rows, :] + edge
        r.goal[cell, rows, :] = total
        return conduct(total, r.factor[cell, rows, :]), total

    heads = {start: k_of(start) for start in STARTS}
    first_k = heads[0][0]
    state = []
    for start in STARTS:
        after, after_side = k_of(start + 1)
        head_k = heads[start][0]
        link = head_k * after / (head_k + after)
        if start == 0:
            head_ground = jnp.ones((8, LANES), jnp.float32)
            head_side = heads[0][1]
        else:
            head_ground = jnp.zeros((8, LANES), jnp.float32)
            head_side = jnp.zeros((8, LANES), jnp.float32)
        state.append(
            (jnp.ones((8, LANES), jnp.float32), link, after_side, head_ground, head_side, after)
        )
    last_k = None
    for offset in range(1, 16):
        for chain, (start, end) in enumerate(zip(STARTS, ENDS)):
            cell = start + offset
            if cell >= end:
                continue
            ground, link, side, head_ground, head_side, k = state[chain]
            after, after_side = heads[cell + 1] if cell + 1 in heads else k_of(cell + 1)
            both = k + after
            product = k * after
            inverse = 1.0 / ((ground + link) * both + product)
            own = both * inverse
            ahead = product * inverse
            back = link * own
            r.to_next[cell, rows, :] = ahead
            r.to_sep[cell, rows, :] = back
            r.base[cell, rows, :] = side * own
            state[chain] = (
                1.0 + ground * ahead,
                link * ahead,
                after_side + side * ahead,
                head_ground + ground * back,
                head_side + side * back,
                after,
            )
            if cell + 1 == CELLS - 1:
                last_k = after
    ground_16 = state[0][0] + state[1][3]
    side_16 = state[0][2] + state[1][4]
    ground_32 = state[1][0] + state[2][3]
    side_32 = state[1][2] + state[2][4]
    ground_48 = state[2][0] + state[3][3]
    side_48 = state[2][2] + state[3][4]
    ground_0, side_0 = state[0][3], state[0][4]
    ground_63, side_63 = state[3][0], state[3][2]
    links = [part[1] for part in state]

    left, right, own = eliminate(ground_16, links[0], links[1], side_16)
    r.to_sep[16, rows, :] = left
    r.to_next[16, rows, :] = right
    r.base[16, rows, :] = own
    ground_0 += ground_16 * left
    side_0 += side_16 * left
    ground_32 += ground_16 * right
    side_32 += side_16 * right
    link_low = links[0] * right

    left, right, own = eliminate(ground_48, links[2], links[3], side_48)
    r.to_sep[48, rows, :] = left
    r.to_next[48, rows, :] = right
    r.base[48, rows, :] = own
    ground_32 += ground_48 * left
    side_32 += side_48 * left
    ground_63 += ground_48 * right
    side_63 += side_48 * right
    link_high = links[2] * right

    left, right, own = eliminate(ground_32, link_low, link_high, side_32)
    r.to_sep[32, rows, :] = left
    r.to_next[32, rows, :] = right
    r.base[32, rows, :] = own
    ground_0 += ground_32 * left
    side_0 += side_32 * left
    ground_63 += ground_32 * right
    side_63 += side_32 * right
    link = link_low * right

    to_face, to_last, own = eliminate(ground_0, first_k, link, side_0)
    r.to_sep[0, rows, :] = to_face
    r.to_next[0, rows, :] = to_last
    r.base[0, rows, :] = own
    ground_low = ground_0 * to_face
    side_low = side_0 * to_face
    ground_63 += ground_0 * to_last
    side_63 += side_0 * to_last
    link = first_k * to_last

    to_low, to_high, own = eliminate(ground_63, link, last_k, side_63)
    r.to_sep[63, rows, :] = to_low
    r.to_next[63, rows, :] = to_high
    r.base[63, rows, :] = own
    ground_low += ground_63 * to_low
    side_low += side_63 * to_low
    link = link * to_high
    faces = (link, ground_low, ground_63 * to_high, side_low, side_63 * to_high)
    for at, value in enumerate(faces):
        r.packet[turn, tile, at] = value


def spread_tile(r, turn, pack_to, tile):
    rows = row_block(tile)
    low_face = r.returned[turn, tile, 0]
    high_face = r.returned[turn, tile, 1]
    lane_pair = lane_at() // 2
    packed = [jnp.zeros((8, LANES), jnp.float32)]

    def value(cell, sep, following):
        return (
            r.base[cell, rows, :]
            + r.to_sep[cell, rows, :] * sep
            + r.to_next[cell, rows, :] * following
        )

    def keep(cell, x):
        r.field[cell, rows, :] = x
        if pack_to is not None:
            packed[0] = jnp.where(lane_pair == cell, pltpu.roll(x, 2 * cell + 1, 1), packed[0])

    x_last = value(63, low_face, high_face)
    x_first = value(0, low_face, x_last)
    x_32 = value(32, x_first, x_last)
    x_16 = value(16, x_first, x_32)
    x_48 = value(48, x_32, x_last)
    seps = {0: x_first, 16: x_16, 32: x_32, 48: x_48, 63: x_last}
    for cell, x in seps.items():
        keep(cell, x)
    later = [seps[end] for end in ENDS]
    for offset in range(15, 0, -1):
        for chain, (start, end) in enumerate(zip(STARTS, ENDS)):
            cell = start + offset
            if cell >= end:
                continue
            later[chain] = value(cell, seps[start], later[chain])
            keep(cell, later[chain])
    if pack_to is not None:
        r.ends[pack_to, rows, :] = packed[0]


def close_ring(r, turn):
    parts = [[r.gathered[turn, member, at] for at in range(VALUES)] for member in range(TILES)]
    count = TILES
    ground = [parts[at][1] + parts[at - 1][2] for at in range(count)]
    side = [parts[at][3] + parts[at - 1][4] for at in range(count)]
    links = [parts[at - 1][0] for at in range(count)]
    undo = []
    nodes = list(range(count))
    while len(nodes) > 2:
        size = len(nodes)
        kept_links = []
        for at in range(1, size, 2):
            node, low, high = nodes[at], nodes[at - 1], nodes[(at + 1) % size]
            to_low, to_high, own = eliminate(ground[node], links[at], links[(at + 1) % size], side[node])
            undo.append((node, low, high, to_low, to_high, own))
            ground[low] = ground[low] + ground[node] * to_low
            side[low] = side[low] + side[node] * to_low
            ground[high] = ground[high] + ground[node] * to_high
            side[high] = side[high] + side[node] * to_high
            kept_links.append(links[at] * to_high)
        nodes = nodes[::2]
        links = kept_links[-1:] + kept_links[:-1]
    low, high = nodes
    link = links[0] + links[1]
    inverse = 1.0 / (ground[high] + link)
    to_low = link * inverse
    x = [None] * count
    x[low] = (side[low] + side[high] * to_low) / (ground[low] + ground[high] * to_low)
    x[high] = side[high] * inverse + to_low * x[low]
    for node, low, high, to_low, to_high, own in reversed(undo):
        x[node] = own + to_low * x[low] + to_high * x[high]
    for member in range(count):
        r.answer[turn, member, 0] = x[member]
        r.answer[turn, member, 1] = x[(member + 1) % count]


NAMES = (
    "field", "factor", "beyond", "supply", "raw", "goal", "to_sep", "to_next", "base",
    "own_field", "own_factor", "own_supply", "scaled", "stage",
    "own_ends", "paired_ends", "halves", "ends", "factor_ends", "near_ends", "near_factor",
    "packet", "gathered", "answer", "returned",
    "load_sem", "move_sem", "swap_send", "swap_recv", "first_send", "first_recv",
    "halo_send", "halo_recv", "packet_send", "packet_recv", "answer_send", "answer_recv",
    "out_sem", "out_send", "out_recv",
)


def kernel(warmth_hbm, factor_hbm, supply_hbm, out_hbm, *refs):
    r = types.SimpleNamespace(**dict(zip(NAMES, refs)))
    az = lax.axis_index("az")
    gz = lax.axis_index("gz")
    core = lax.rem(az, 2)
    chip = az // 2
    sibling = az + 1 - 2 * core
    gz_count = lax.axis_size("gz")
    across = gz + 1 - 2 * lax.rem(gz, 2)
    gz_up = lax.rem(gz + 1, gz_count)
    gz_down = lax.rem(gz + gz_count - 1, gz_count)
    other = lax.rem(gz + gz_count - 1 + 2 * lax.rem(gz, 2), gz_count)
    low_gz = jnp.where(gz > 0, 1.0, 0.0)
    high_gz = jnp.where(gz < gz_count - 1, 1.0, 0.0)

    barrier = pltpu.get_barrier_semaphore()
    for member in range(TILES):
        pl.semaphore_signal(
            barrier, inc=1, device_id=(2 * member + 1 - core, across), device_id_type=MESH
        )
    for where in ((sibling, gz), (az, across), (az, other), (sibling, other)):
        pl.semaphore_signal(barrier, inc=1, device_id=where, device_id_type=MESH)

    def for_range(low, high, work):
        def one(at, carry):
            work(at)
            return carry

        lax.fori_loop(low, high, one, 0)

    def remote(source, target, send_sem, recv_sem, where):
        return pltpu.make_async_remote_copy(
            src_ref=source, dst_ref=target, send_sem=send_sem, recv_sem=recv_sem,
            device_id=where, device_id_type=MESH,
        )

    def wait_for(ref, sem):
        pltpu.make_async_copy(ref, ref, sem).wait()

    loads = ((warmth_hbm, r.own_field), (factor_hbm, r.own_factor), (supply_hbm, r.own_supply))

    def load(cell):
        for at, (source, target) in enumerate(loads):
            pltpu.make_async_copy(source.at[:, cell], target.at[cell], r.load_sem.at[at]).start()

    for_range(0, HALF, load)
    for at in range(2):
        wait_for(loads[at][1], r.load_sem.at[at])

    own_rows = pl.ds(core * ROWS, ROWS)
    sent_rows = pl.ds((1 - core) * ROWS, ROWS)
    own_cells = pl.ds(core * HALF, HALF)
    sent_tile = (1 - core) * TILES
    own_tile = core * TILES

    for_range(sent_tile, sent_tile + TILES, functools.partial(prepare, r, core))
    pl.semaphore_wait(barrier, TILES + 4)
    factor_swap = remote(
        r.scaled.at[:, sent_rows], r.factor.at[own_cells],
        r.swap_send.at[0], r.swap_recv.at[0], (sibling, gz),
    )
    factor_swap.start()
    for_range(own_tile, own_tile + TILES, functools.partial(prepare, r, core))
    factor_move = pltpu.make_async_copy(
        r.scaled.at[:, own_rows], r.factor.at[own_cells], r.move_sem.at[0]
    )
    factor_move.start()
    firsts = []
    for side, where in enumerate((gz_down, gz_up)):
        for same in range(2):
            firsts.append(
                remote(
                    r.own_ends.at[:, own_rows if same else sent_rows],
                    r.halves.at[side, core],
                    r.first_send.at[2 * side + same],
                    r.first_recv.at[2 * side + core],
                    (az if same else sibling, where),
                )
            )
    firsts.append(
        remote(
            r.own_ends.at[:, sent_rows], r.paired_ends,
            r.first_send.at[4], r.first_recv.at[4], (sibling, gz),
        )
    )
    for copy in firsts:
        copy.start()
    wait_for(r.own_supply, r.load_sem.at[2])

    goal_swaps = []
    for chunk in range(2):
        low = sent_tile + PART * chunk
        for_range(
            low, low + PART,
            functools.partial(explicit_first, r, r.stage, 0, sent_tile * 8),
        )
        rows = pl.ds(PART * 8 * chunk, PART * 8)
        goal_swaps.append(
            remote(
                r.stage.at[:, rows], r.raw.at[own_cells, rows],
                r.swap_send.at[1 + chunk], r.swap_recv.at[1 + chunk], (sibling, gz),
            )
        )
        goal_swaps[-1].start()
    supply_swap = remote(
        r.own_supply.at[:, sent_rows], r.supply.at[own_cells],
        r.swap_send.at[3], r.swap_recv.at[3], (sibling, gz),
    )
    supply_swap.start()
    supply_move = pltpu.make_async_copy(
        r.own_supply.at[:, own_rows], r.supply.at[own_cells], r.move_sem.at[1]
    )
    supply_move.start()
    for_range(
        own_tile, own_tile + TILES,
        functools.partial(explicit_first, r, r.raw, core * HALF, own_tile * 8),
    )
    for side in range(2):
        for source in range(2):
            wait_for(r.halves.at[side, source], r.first_recv.at[2 * side + source])
    wait_for(r.paired_ends, r.first_recv.at[4])
    for_range(0, TILES, functools.partial(merge, r, core))
    factor_move.wait()
    factor_swap.wait_recv()

    y_at = lax.rem(chip, 4)

    def wrap(shift):
        return jnp.where(y_at + shift >= 4, y_at + shift - 4, y_at + shift)

    seats = [wrap(2), wrap(1), wrap(3), y_at]

    def ordered(chunk, at):
        first = jnp.where(at == 0, seats[0], seats[1])
        return PART * chunk + jnp.where(at < 2, first, jnp.where(at == 2, seats[2], seats[3]))

    def forward(step, picard, chunk):
        turn = PICARD * step + picard

        def work(at):
            tile = ordered(chunk, at)
            border = None if picard else border_of(r, core, low_gz, high_gz, step, tile)
            reduce_tile(r, border, turn, tile)
            remote(
                r.packet.at[turn, tile], r.gathered.at[turn, chip],
                r.packet_send.at[turn], r.packet_recv.at[turn], (2 * tile + 1 - core, across),
            ).start()

        for_range(0, PART, work)

    def solve(turn):
        wait_for(r.gathered.at[turn], r.packet_recv.at[turn])
        close_ring(r, turn)

        for seat in seats:
            for half in range(2):
                member = seat + 4 * half
                remote(
                    r.answer.at[turn, member], r.returned.at[turn, chip],
                    r.answer_send.at[turn], r.answer_recv.at[turn, chip],
                    (2 * member + 1 - core, across),
                ).start()

    def backward(turn, chunk, pack_to):
        def work(at):
            tile = ordered(chunk, PART - 1 - at)
            wait_for(r.returned.at[turn, tile], r.answer_recv.at[turn, tile])
            spread_tile(r, turn, pack_to, tile)

        for_range(0, PART, work)

    def unload(chunk):
        rows = pl.ds(PART * 8 * chunk, PART * 8)
        placed = pl.ds(core * ROWS + PART * 8 * chunk, PART * 8)

        def one(cell):
            target = out_hbm.at[placed, cell]
            remote(
                r.field.at[(1 - core) * HALF + cell, rows], target,
                r.out_send, r.out_recv, (sibling, gz),
            ).start()
            pltpu.make_async_copy(
                r.field.at[core * HALF + cell, rows], target, r.out_sem
            ).start()

        for_range(0, HALF, one)

    halos = [[], []]
    for step in range(STEPS):
        for chunk in range(2):
            rows = pl.ds(PART * 8 * chunk, PART * 8)
            if step == 0:
                goal_swaps[chunk].wait_recv()
            else:
                low = PART * chunk
                for_range(low, low + PART, functools.partial(explicit_later, r, core))
                for copy in halos[chunk]:
                    copy.wait()
            forward(step, 0, chunk)
        if step == 0:
            for_range(0, TILES, functools.partial(shift_factor, r))
        for picard in range(PICARD):
            turn = PICARD * step + picard
            final = picard == PICARD - 1
            solve(turn)
            for chunk in range(2):
                last = step == STEPS - 1
                backward(turn, chunk, step + 1 if final and not last else None)
                if not final:
                    forward(step, picard + 1, chunk)
                elif last:
                    unload(chunk)
                else:
                    rows = pl.ds(PART * 8 * chunk, PART * 8)
                    for side, where in enumerate((gz_down, gz_up)):
                        copy = remote(
                            r.ends.at[step + 1, rows], r.near_ends.at[step + 1, side, rows],
                            r.halo_send.at[chunk, side], r.halo_recv.at[chunk, side],
                            (az, where),
                        )
                        copy.start()
                        halos[chunk].append(copy)
        if step == 0:
            supply_swap.wait_recv()
            supply_move.wait()

    for copy in [factor_swap, supply_swap] + goal_swaps + firsts:
        copy.wait_send()
    for turn in range(STEPS * PICARD):
        wait_for(r.packet.at[turn], r.packet_send.at[turn])
        wait_for(r.answer.at[turn], r.answer_send.at[turn])
    whole = r.field.at[pl.ds(0, HALF)]
    wait_for(whole, r.out_sem)
    wait_for(whole, r.out_send)
    wait_for(whole, r.out_recv)


def shards(starting_warmth, volume_transfer_multiplier, energy_supply_history):
    def real(*shape):
        return pltpu.VMEM(shape + (LANES,), jnp.float32)

    cells = real(CELLS, ROWS)
    own = real(HALF, 2 * ROWS)
    dma = pltpu.SemaphoreType.DMA
    turns = STEPS * PICARD
    anywhere = pl.BlockSpec(memory_space=pltpu.HBM)
    return pl.pallas_call(
        kernel,
        out_shape=jax.ShapeDtypeStruct(starting_warmth.shape, jnp.float32),
        in_specs=[anywhere] * 3,
        out_specs=anywhere,
        scratch_shapes=[cells] * 9 + [own] * 4 + [
            real(HALF, ROWS),
            real(2, 2 * ROWS), real(2, ROWS), real(2, 2, 2, ROWS), real(STEPS, ROWS),
            real(ROWS), real(STEPS, 2, ROWS), real(2, ROWS),
            real(turns, TILES, VALUES, 8), real(turns, TILES, VALUES, 8),
            real(turns, TILES, 2, 8), real(turns, TILES, 2, 8),
            dma((3,)), dma((2,)), dma((4,)), dma((4,)), dma((5,)), dma((5,)),
            dma((2, 2)), dma((2, 2)),
            dma((turns,)), dma((turns,)), dma((turns,)), dma((turns, TILES)),
            dma, dma, dma,
        ],
        compiler_params=pltpu.CompilerParams(
            collective_id=0, has_side_effects=True, vmem_limit_bytes=60 * 1024 * 1024
        ),
        name="annulus",
    )(starting_warmth, volume_transfer_multiplier, energy_supply_history)


def solution(mesh):
    placed = (P(None, "az", "gz"), P(None, "az", "gz"), P(None, "az", "gz"))
    return jax.shard_map(
        shards, mesh=mesh, in_specs=placed, out_specs=P(None, "az", "gz"), check_vma=False
    )
```

```python
import functools
import types

import jax
import jax.numpy as jnp
from jax import lax
from jax.experimental import pallas as pl
from jax.experimental.pallas import tpu as pltpu
from jax.sharding import PartitionSpec as P

STEPS = 2
PICARD = 2
diffusion_number = 1000.0
lengthwise_ratio = 0.048

MESH = pl.DeviceIdType.MESH
CELLS = 64
HALF = 32
ROWS = 64
TILES = 8
PART = 4
LANES = 128
VALUES = 5
GROUP = 16
STARTS = (0, 16, 32, 48)
ENDS = (16, 32, 48, 63)


def row_block(tile):
    return pl.ds(pl.multiple_of(tile * 8, 8), 8)


def conduct(field, factor):
    return factor * (1.5 + jnp.tanh(field))


def eliminate(ground, left, right, side):
    inverse = 1.0 / (ground + left + right)
    to_left = left * inverse
    to_right = right * inverse
    return to_left, to_right, side * inverse


def lane_at():
    return lax.broadcasted_iota(jnp.int32, (8, LANES), 1)


def twice_number(core, tile):
    rows = (lax.broadcasted_iota(jnp.int32, (8, LANES), 0) + (core * ROWS + tile * 8)).astype(jnp.float32)
    ratio = 128.0 / (128.0 + rows)
    return (2.0 * diffusion_number) * (ratio * ratio)


def first_rows(tile):
    rows = (lax.broadcasted_iota(jnp.int32, (8, LANES), 0) + tile * 8).astype(jnp.float32)
    ratio = 128.0 / (128.0 + rows)
    return (2.0 * diffusion_number) * (ratio * ratio)


def prepare(r, core, tile):
    rows = row_block(tile)
    lane_pair = lane_at() // 2
    number = first_rows(tile)
    packed = jnp.zeros((8, LANES), jnp.float32)
    packed_factor = jnp.zeros((8, LANES), jnp.float32)
    for cell in range(HALF):
        here = lane_pair == cell
        scaled = r.own_factor[cell, rows, :] * number
        r.scaled[cell, rows, :] = scaled
        packed = jnp.where(here, pltpu.roll(r.own_field[cell, rows, :], 2 * cell + 1, 1), packed)
        packed_factor = jnp.where(here, pltpu.roll(scaled, 2 * cell + 1, 1), packed_factor)
    r.own_ends[0, rows, :] = jnp.where(core == 0, packed, pltpu.roll(packed, 64, 1))
    r.own_ends[1, rows, :] = jnp.where(core == 0, packed_factor, pltpu.roll(packed_factor, 64, 1))


def merge(r, core, tile):
    rows = row_block(tile)
    low = lane_at() < 64
    ours = jnp.where(core == 0, jnp.where(low, 1, 0), jnp.where(low, 0, 1)) == 1
    held = pl.ds(pl.multiple_of(core * ROWS + tile * 8, 8), 8)
    r.ends[0, rows, :] = jnp.where(ours, r.own_ends[0, held, :], r.paired_ends[0, rows, :])
    r.factor_ends[rows, :] = jnp.where(ours, r.own_ends[1, held, :], r.paired_ends[1, rows, :])
    for side in range(2):
        r.near_ends[0, side, rows, :] = jnp.where(
            low, r.halves[side, 0, 0, rows, :], r.halves[side, 1, 0, rows, :]
        )
        r.near_factor[side, rows, :] = jnp.where(
            low, r.halves[side, 0, 1, rows, :], r.halves[side, 1, 1, rows, :]
        )


def border_of(r, core, low_gz, high_gz, step, tile):
    rows = row_block(tile)
    rate = (2.0 * lengthwise_ratio) / twice_number(core, tile)
    even = lax.rem(lane_at(), 2) == 0
    inside = jnp.where(even, high_gz, low_gz)
    ours = r.ends[step, rows, :]
    near = jnp.where(
        even,
        pltpu.roll(r.near_ends[step, 0, rows, :], LANES - 1, 1),
        pltpu.roll(r.near_ends[step, 1, rows, :], 1, 1),
    )
    near_factor = jnp.where(
        even,
        pltpu.roll(r.near_factor[0, rows, :], LANES - 1, 1),
        pltpu.roll(r.near_factor[1, rows, :], 1, 1),
    )
    our_k = conduct(ours, r.factor_ends[rows, :])
    near_k = conduct(near, near_factor)
    return rate * inside * our_k * near_k / (our_k + near_k) * (near - ours)


def explicit(number, field, factor, beyond, supply, rows, cells, store):
    rate = (2.0 * lengthwise_ratio) / number
    last = lane_at() == LANES - 1
    for group in range(0, cells, GROUP):
        at = range(group, group + GROUP)
        here = [field[cell, rows, :] for cell in at]
        k = [conduct(x, factor[cell, rows, :]) for cell, x in zip(at, here)]
        above = [pltpu.roll(x, LANES - 1, 1) for x in here]
        if beyond is None:
            k_above = [pltpu.roll(x, LANES - 1, 1) for x in k]
        else:
            k_above = [conduct(x, beyond[cell, rows, :]) for cell, x in zip(at, above)]
        flux = [
            jnp.where(last, 0.0, rate * k[i] * k_above[i] / (k[i] + k_above[i]) * (above[i] - here[i]))
            for i in range(GROUP)
        ]
        below = [pltpu.roll(x, 1, 1) for x in flux]
        for i, cell in enumerate(at):
            store(cell, here[i] + (flux[i] - below[i]) + supply[cell, rows, :])


def explicit_first(r, target, base, row_shift, tile):
    rows = row_block(tile)
    placed = pl.ds(pl.multiple_of(tile * 8 - row_shift, 8), 8)

    def store(cell, value):
        target[base + cell, placed, :] = value

    explicit(first_rows(tile), r.own_field, r.scaled, None, r.own_supply, rows, HALF, store)


def explicit_later(r, core, tile):
    rows = row_block(tile)

    def store(cell, value):
        r.raw[cell, rows, :] = value

    explicit(
        twice_number(core, tile), r.field, r.factor, r.beyond, r.supply, rows, CELLS, store
    )


def shift_factor(r, tile):
    rows = row_block(tile)
    for cell in range(CELLS):
        r.beyond[cell, rows, :] = pltpu.roll(r.factor[cell, rows, :], LANES - 1, 1)


def reduce_tile(r, border, turn, tile):
    rows = row_block(tile)
    lane = lane_at()
    rim = jnp.logical_or(lane == 0, lane == LANES - 1)

    def k_of(cell):
        if border is None:
            return conduct(r.field[cell, rows, :], r.factor[cell, rows, :]), r.goal[cell, rows, :]
        edge = jnp.where(rim, pltpu.roll(border, LANES - 1 - 2 * cell, 1), 0.0)
        total = r.raw[cell, rows, :] + edge
        r.goal[cell, rows, :] = total
        return conduct(total, r.factor[cell, rows, :]), total

    heads = {start: k_of(start) for start in STARTS}
    first_k = heads[0][0]
    state = []
    for start in STARTS:
        after, after_side = k_of(start + 1)
        head_k = heads[start][0]
        link = head_k * after / (head_k + after)
        if start == 0:
            head_ground = jnp.ones((8, LANES), jnp.float32)
            head_side = heads[0][1]
        else:
            head_ground = jnp.zeros((8, LANES), jnp.float32)
            head_side = jnp.zeros((8, LANES), jnp.float32)
        state.append(
            (jnp.ones((8, LANES), jnp.float32), link, after_side, head_ground, head_side, after)
        )
    last_k = None
    for offset in range(1, 16):
        for chain, (start, end) in enumerate(zip(STARTS, ENDS)):
            cell = start + offset
            if cell >= end:
                continue
            ground, link, side, head_ground, head_side, k = state[chain]
            after, after_side = heads[cell + 1] if cell + 1 in heads else k_of(cell + 1)
            both = k + after
            product = k * after
            inverse = 1.0 / ((ground + link) * both + product)
            own = both * inverse
            ahead = product * inverse
            back = link * own
            r.to_next[cell, rows, :] = ahead
            r.to_sep[cell, rows, :] = back
            r.base[cell, rows, :] = side * own
            state[chain] = (
                1.0 + ground * ahead,
                link * ahead,
                after_side + side * ahead,
                head_ground + ground * back,
                head_side + side * back,
                after,
            )
            if cell + 1 == CELLS - 1:
                last_k = after
    ground_16 = state[0][0] + state[1][3]
    side_16 = state[0][2] + state[1][4]
    ground_32 = state[1][0] + state[2][3]
    side_32 = state[1][2] + state[2][4]
    ground_48 = state[2][0] + state[3][3]
    side_48 = state[2][2] + state[3][4]
    ground_0, side_0 = state[0][3], state[0][4]
    ground_63, side_63 = state[3][0], state[3][2]
    links = [part[1] for part in state]

    left, right, own = eliminate(ground_16, links[0], links[1], side_16)
    r.to_sep[16, rows, :] = left
    r.to_next[16, rows, :] = right
    r.base[16, rows, :] = own
    ground_0 += ground_16 * left
    side_0 += side_16 * left
    ground_32 += ground_16 * right
    side_32 += side_16 * right
    link_low = links[0] * right

    left, right, own = eliminate(ground_48, links[2], links[3], side_48)
    r.to_sep[48, rows, :] = left
    r.to_next[48, rows, :] = right
    r.base[48, rows, :] = own
    ground_32 += ground_48 * left
    side_32 += side_48 * left
    ground_63 += ground_48 * right
    side_63 += side_48 * right
    link_high = links[2] * right

    left, right, own = eliminate(ground_32, link_low, link_high, side_32)
    r.to_sep[32, rows, :] = left
    r.to_next[32, rows, :] = right
    r.base[32, rows, :] = own
    ground_0 += ground_32 * left
    side_0 += side_32 * left
    ground_63 += ground_32 * right
    side_63 += side_32 * right
    link = link_low * right

    to_face, to_last, own = eliminate(ground_0, first_k, link, side_0)
    r.to_sep[0, rows, :] = to_face
    r.to_next[0, rows, :] = to_last
    r.base[0, rows, :] = own
    ground_low = ground_0 * to_face
    side_low = side_0 * to_face
    ground_63 += ground_0 * to_last
    side_63 += side_0 * to_last
    link = first_k * to_last

    to_low, to_high, own = eliminate(ground_63, link, last_k, side_63)
    r.to_sep[63, rows, :] = to_low
    r.to_next[63, rows, :] = to_high
    r.base[63, rows, :] = own
    ground_low += ground_63 * to_low
    side_low += side_63 * to_low
    link = link * to_high
    faces = (link, ground_low, ground_63 * to_high, side_low, side_63 * to_high)
    for at, value in enumerate(faces):
        r.packet[turn, tile, at] = value


def spread_tile(r, turn, pack_to, tile):
    rows = row_block(tile)
    low_face = r.returned[turn, tile, 0]
    high_face = r.returned[turn, tile, 1]
    lane_pair = lane_at() // 2
    packed = [jnp.zeros((8, LANES), jnp.float32)]

    def value(cell, sep, following):
        return (
            r.base[cell, rows, :]
            + r.to_sep[cell, rows, :] * sep
            + r.to_next[cell, rows, :] * following
        )

    def keep(cell, x):
        r.field[cell, rows, :] = x
        if pack_to is not None:
            packed[0] = jnp.where(lane_pair == cell, pltpu.roll(x, 2 * cell + 1, 1), packed[0])

    x_last = value(63, low_face, high_face)
    x_first = value(0, low_face, x_last)
    x_32 = value(32, x_first, x_last)
    x_16 = value(16, x_first, x_32)
    x_48 = value(48, x_32, x_last)
    seps = {0: x_first, 16: x_16, 32: x_32, 48: x_48, 63: x_last}
    for cell, x in seps.items():
        keep(cell, x)
    later = [seps[end] for end in ENDS]
    for offset in range(15, 0, -1):
        for chain, (start, end) in enumerate(zip(STARTS, ENDS)):
            cell = start + offset
            if cell >= end:
                continue
            later[chain] = value(cell, seps[start], later[chain])
            keep(cell, later[chain])
    if pack_to is not None:
        r.ends[pack_to, rows, :] = packed[0]


def close_ring(r, turn, chunk):
    parts = [[r.gathered[turn, chunk, member, at] for at in range(VALUES)] for member in range(TILES)]
    count = TILES
    ground = [parts[at][1] + parts[at - 1][2] for at in range(count)]
    side = [parts[at][3] + parts[at - 1][4] for at in range(count)]
    links = [parts[at - 1][0] for at in range(count)]
    undo = []
    nodes = list(range(count))
    while len(nodes) > 2:
        size = len(nodes)
        kept_links = []
        for at in range(1, size, 2):
            node, low, high = nodes[at], nodes[at - 1], nodes[(at + 1) % size]
            to_low, to_high, own = eliminate(ground[node], links[at], links[(at + 1) % size], side[node])
            undo.append((node, low, high, to_low, to_high, own))
            ground[low] = ground[low] + ground[node] * to_low
            side[low] = side[low] + side[node] * to_low
            ground[high] = ground[high] + ground[node] * to_high
            side[high] = side[high] + side[node] * to_high
            kept_links.append(links[at] * to_high)
        nodes = nodes[::2]
        links = kept_links[-1:] + kept_links[:-1]
    low, high = nodes
    link = links[0] + links[1]
    inverse = 1.0 / (ground[high] + link)
    to_low = link * inverse
    x = [None] * count
    x[low] = (side[low] + side[high] * to_low) / (ground[low] + ground[high] * to_low)
    x[high] = side[high] * inverse + to_low * x[low]
    for node, low, high, to_low, to_high, own in reversed(undo):
        x[node] = own + to_low * x[low] + to_high * x[high]
    for member in range(count):
        r.answer[turn, chunk, member, 0] = x[member]
        r.answer[turn, chunk, member, 1] = x[(member + 1) % count]


NAMES = (
    "field", "factor", "beyond", "supply", "raw", "goal", "to_sep", "to_next", "base",
    "own_field", "own_factor", "own_supply", "scaled", "stage",
    "own_ends", "paired_ends", "halves", "ends", "factor_ends", "near_ends", "near_factor",
    "packet", "gathered", "answer", "returned",
    "load_sem", "move_sem", "swap_send", "swap_recv", "first_send", "first_recv",
    "halo_send", "halo_recv", "packet_send", "packet_recv", "answer_send", "answer_recv",
    "out_sem", "out_send", "out_recv",
)


def kernel(warmth_hbm, factor_hbm, supply_hbm, out_hbm, *refs):
    r = types.SimpleNamespace(**dict(zip(NAMES, refs)))
    az = lax.axis_index("az")
    gz = lax.axis_index("gz")
    core = lax.rem(az, 2)
    chip = az // 2
    sibling = az + 1 - 2 * core
    gz_count = lax.axis_size("gz")
    across = gz + 1 - 2 * lax.rem(gz, 2)
    gz_up = lax.rem(gz + 1, gz_count)
    gz_down = lax.rem(gz + gz_count - 1, gz_count)
    other = lax.rem(gz + gz_count - 1 + 2 * lax.rem(gz, 2), gz_count)
    low_gz = jnp.where(gz > 0, 1.0, 0.0)
    high_gz = jnp.where(gz < gz_count - 1, 1.0, 0.0)

    barrier = pltpu.get_barrier_semaphore()
    for member in range(TILES):
        pl.semaphore_signal(
            barrier, inc=1, device_id=(2 * member + 1 - core, across), device_id_type=MESH
        )
    for where in ((sibling, gz), (az, across), (az, other), (sibling, other)):
        pl.semaphore_signal(barrier, inc=1, device_id=where, device_id_type=MESH)

    def for_range(low, high, work):
        def one(at, carry):
            work(at)
            return carry

        lax.fori_loop(low, high, one, 0)

    def remote(source, target, send_sem, recv_sem, where):
        return pltpu.make_async_remote_copy(
            src_ref=source, dst_ref=target, send_sem=send_sem, recv_sem=recv_sem,
            device_id=where, device_id_type=MESH,
        )

    def wait_for(ref, sem):
        pltpu.make_async_copy(ref, ref, sem).wait()

    loads = ((warmth_hbm, r.own_field), (factor_hbm, r.own_factor), (supply_hbm, r.own_supply))

    def load(arrays, cell):
        for at in arrays:
            source, target = loads[at]
            pltpu.make_async_copy(source.at[:, cell], target.at[cell], r.load_sem.at[at]).start()

    for_range(0, HALF, functools.partial(load, (0, 1)))
    for_range(0, HALF, functools.partial(load, (2,)))
    for at in range(2):
        wait_for(loads[at][1], r.load_sem.at[at])

    own_rows = pl.ds(core * ROWS, ROWS)
    sent_rows = pl.ds((1 - core) * ROWS, ROWS)
    own_cells = pl.ds(core * HALF, HALF)
    sent_tile = (1 - core) * TILES
    own_tile = core * TILES

    for_range(sent_tile, sent_tile + TILES, functools.partial(prepare, r, core))
    pl.semaphore_wait(barrier, TILES + 4)
    factor_swap = remote(
        r.scaled.at[:, sent_rows], r.factor.at[own_cells],
        r.swap_send.at[0], r.swap_recv.at[0], (sibling, gz),
    )
    factor_swap.start()
    for_range(own_tile, own_tile + TILES, functools.partial(prepare, r, core))
    factor_move = pltpu.make_async_copy(
        r.scaled.at[:, own_rows], r.factor.at[own_cells], r.move_sem.at[0]
    )
    factor_move.start()
    firsts = []
    for side, where in enumerate((gz_down, gz_up)):
        for same in range(2):
            firsts.append(
                remote(
                    r.own_ends.at[:, own_rows if same else sent_rows],
                    r.halves.at[side, core],
                    r.first_send.at[2 * side + same],
                    r.first_recv.at[2 * side + core],
                    (az if same else sibling, where),
                )
            )
    firsts.append(
        remote(
            r.own_ends.at[:, sent_rows], r.paired_ends,
            r.first_send.at[4], r.first_recv.at[4], (sibling, gz),
        )
    )
    for copy in firsts:
        copy.start()
    wait_for(r.own_supply, r.load_sem.at[2])

    goal_swaps = []
    for chunk in range(2):
        low = sent_tile + PART * chunk
        for_range(
            low, low + PART,
            functools.partial(explicit_first, r, r.stage, 0, sent_tile * 8),
        )
        rows = pl.ds(PART * 8 * chunk, PART * 8)
        goal_swaps.append(
            remote(
                r.stage.at[:, rows], r.raw.at[own_cells, rows],
                r.swap_send.at[1 + chunk], r.swap_recv.at[1 + chunk], (sibling, gz),
            )
        )
        goal_swaps[-1].start()
    supply_swap = remote(
        r.own_supply.at[:, sent_rows], r.supply.at[own_cells],
        r.swap_send.at[3], r.swap_recv.at[3], (sibling, gz),
    )
    supply_swap.start()
    supply_move = pltpu.make_async_copy(
        r.own_supply.at[:, own_rows], r.supply.at[own_cells], r.move_sem.at[1]
    )
    supply_move.start()
    for_range(
        own_tile, own_tile + TILES,
        functools.partial(explicit_first, r, r.raw, core * HALF, own_tile * 8),
    )
    for side in range(2):
        for source in range(2):
            wait_for(r.halves.at[side, source], r.first_recv.at[2 * side + source])
    wait_for(r.paired_ends, r.first_recv.at[4])
    for_range(0, TILES, functools.partial(merge, r, core))
    factor_move.wait()
    factor_swap.wait_recv()

    y_at = lax.rem(chip, 4)

    def wrap(shift):
        return jnp.where(y_at + shift >= 4, y_at + shift - 4, y_at + shift)

    seats = [wrap(2), wrap(1), wrap(3), y_at]

    layer = lax.rem(gz, 2)
    solves = chip // 4 == 1 - layer

    def ordered(at):
        first = jnp.where(at == 0, seats[0], seats[1])
        return jnp.where(at < 2, first, jnp.where(at == 2, seats[2], seats[3]))

    def forward(step, picard, chunk):
        turn = PICARD * step + picard

        def work(at):
            seat = ordered(at)
            tile = PART * chunk + seat
            border = None if picard else border_of(r, core, low_gz, high_gz, step, tile)
            reduce_tile(r, border, turn, tile)
            remote(
                r.packet.at[turn, tile], r.gathered.at[turn, chunk, chip],
                r.packet_send.at[turn], r.packet_recv.at[turn, chunk],
                (2 * (4 * layer + seat) + 1 - core, across),
            ).start()

        for_range(0, PART, work)

    def solve(turn):
        @pl.when(solves)
        def _():
            for chunk in range(2):
                wait_for(r.gathered.at[turn, chunk], r.packet_recv.at[turn, chunk])
                close_ring(r, turn, chunk)
                tile = PART * chunk + y_at
                for seat in seats:
                    for half in range(2):
                        member = seat + 4 * half
                        remote(
                            r.answer.at[turn, chunk, member], r.returned.at[turn, tile],
                            r.answer_send.at[turn], r.answer_recv.at[turn, tile],
                            (2 * member + 1 - core, across),
                        ).start()

    def backward(turn, chunk, pack_to):
        def work(at):
            tile = PART * chunk + ordered(PART - 1 - at)
            wait_for(r.returned.at[turn, tile], r.answer_recv.at[turn, tile])
            spread_tile(r, turn, pack_to, tile)

        for_range(0, PART, work)

    def unload(chunk):
        rows = pl.ds(PART * 8 * chunk, PART * 8)
        placed = pl.ds(core * ROWS + PART * 8 * chunk, PART * 8)

        def to_sibling(cell):
            remote(
                r.field.at[(1 - core) * HALF + cell, rows], out_hbm.at[placed, cell],
                r.out_send, r.out_recv, (sibling, gz),
            ).start()

        def to_own(cell):
            pltpu.make_async_copy(
                r.field.at[core * HALF + cell, rows], out_hbm.at[placed, cell], r.out_sem
            ).start()

        for_range(0, HALF, to_sibling)
        for_range(0, HALF, to_own)

    halos = [[], []]
    for step in range(STEPS):
        for chunk in range(2):
            rows = pl.ds(PART * 8 * chunk, PART * 8)
            if step == 0:
                goal_swaps[chunk].wait_recv()
            else:
                low = PART * chunk
                for_range(low, low + PART, functools.partial(explicit_later, r, core))
                for copy in halos[chunk]:
                    copy.wait()
            forward(step, 0, chunk)
        if step == 0:
            for_range(0, TILES, functools.partial(shift_factor, r))
        for picard in range(PICARD):
            turn = PICARD * step + picard
            final = picard == PICARD - 1
            solve(turn)
            for chunk in range(2):
                last = step == STEPS - 1
                backward(turn, chunk, step + 1 if final and not last else None)
                if not final:
                    forward(step, picard + 1, chunk)
                elif last:
                    unload(chunk)
                else:
                    rows = pl.ds(PART * 8 * chunk, PART * 8)
                    for side, where in enumerate((gz_down, gz_up)):
                        copy = remote(
                            r.ends.at[step + 1, rows], r.near_ends.at[step + 1, side, rows],
                            r.halo_send.at[chunk, side], r.halo_recv.at[chunk, side],
                            (az, where),
                        )
                        copy.start()
                        halos[chunk].append(copy)
        if step == 0:
            supply_swap.wait_recv()
            supply_move.wait()

    for copy in [factor_swap, supply_swap] + goal_swaps + firsts:
        copy.wait_send()
    for turn in range(STEPS * PICARD):
        wait_for(r.packet.at[turn], r.packet_send.at[turn])

    @pl.when(solves)
    def _():
        for turn in range(STEPS * PICARD):
            wait_for(r.answer.at[turn], r.answer_send.at[turn])

    whole = r.field.at[pl.ds(0, HALF)]
    wait_for(whole, r.out_sem)
    wait_for(whole, r.out_send)
    wait_for(whole, r.out_recv)


def shards(starting_warmth, volume_transfer_multiplier, energy_supply_history):
    def real(*shape):
        return pltpu.VMEM(shape + (LANES,), jnp.float32)

    cells = real(CELLS, ROWS)
    own = real(HALF, 2 * ROWS)
    dma = pltpu.SemaphoreType.DMA
    turns = STEPS * PICARD
    anywhere = pl.BlockSpec(memory_space=pltpu.HBM)
    return pl.pallas_call(
        kernel,
        out_shape=jax.ShapeDtypeStruct(starting_warmth.shape, jnp.float32),
        in_specs=[anywhere] * 3,
        out_specs=anywhere,
        scratch_shapes=[cells] * 9 + [own] * 4 + [
            real(HALF, ROWS),
            real(2, 2 * ROWS), real(2, ROWS), real(2, 2, 2, ROWS), real(STEPS, ROWS),
            real(ROWS), real(STEPS, 2, ROWS), real(2, ROWS),
            real(turns, TILES, VALUES, 8), real(turns, 2, TILES, VALUES, 8),
            real(turns, 2, TILES, 2, 8), real(turns, TILES, 2, 8),
            dma((3,)), dma((2,)), dma((4,)), dma((4,)), dma((5,)), dma((5,)),
            dma((2, 2)), dma((2, 2)),
            dma((turns,)), dma((turns, 2)), dma((turns,)), dma((turns, TILES)),
            dma, dma, dma,
        ],
        compiler_params=pltpu.CompilerParams(
            collective_id=0, has_side_effects=True, vmem_limit_bytes=60 * 1024 * 1024
        ),
        name="annulus",
    )(starting_warmth, volume_transfer_multiplier, energy_supply_history)


def solution(mesh):
    placed = (P(None, "az", "gz"), P(None, "az", "gz"), P(None, "az", "gz"))
    return jax.shard_map(
        shards, mesh=mesh, in_specs=placed, out_specs=P(None, "az", "gz"), check_vma=False
    )
```

```python
import functools
import types

import jax
import jax.numpy as jnp
from jax import lax
from jax.experimental import pallas as pl
from jax.experimental.pallas import tpu as pltpu
from jax.sharding import PartitionSpec as P

STEPS = 2
PICARD = 2
diffusion_number = 1000.0
lengthwise_ratio = 0.048

MESH = pl.DeviceIdType.MESH
CELLS = 64
HALF = 32
ROWS = 64
TILES = 8
PART = 4
LANES = 128
VALUES = 5
GROUP = 16
STARTS = (0, 16, 32, 48)
ENDS = (16, 32, 48, 63)


def row_block(tile):
    return pl.ds(pl.multiple_of(tile * 8, 8), 8)


def conduct(field, factor):
    return factor * (1.5 + jnp.tanh(field))


def eliminate(ground, left, right, side):
    inverse = 1.0 / (ground + left + right)
    to_left = left * inverse
    to_right = right * inverse
    return to_left, to_right, side * inverse


def lane_at():
    return lax.broadcasted_iota(jnp.int32, (8, LANES), 1)


def twice_number(core, tile):
    rows = (lax.broadcasted_iota(jnp.int32, (8, LANES), 0) + (core * ROWS + tile * 8)).astype(jnp.float32)
    ratio = 128.0 / (128.0 + rows)
    return (2.0 * diffusion_number) * (ratio * ratio)


def first_rows(tile):
    rows = (lax.broadcasted_iota(jnp.int32, (8, LANES), 0) + tile * 8).astype(jnp.float32)
    ratio = 128.0 / (128.0 + rows)
    return (2.0 * diffusion_number) * (ratio * ratio)


def prepare(r, core, tile):
    rows = row_block(tile)
    lane_pair = lane_at() // 2
    number = first_rows(tile)
    packed = jnp.zeros((8, LANES), jnp.float32)
    packed_factor = jnp.zeros((8, LANES), jnp.float32)
    for cell in range(HALF):
        here = lane_pair == cell
        scaled = r.own_factor[cell, rows, :] * number
        r.scaled[cell, rows, :] = scaled
        packed = jnp.where(here, pltpu.roll(r.own_field[cell, rows, :], 2 * cell + 1, 1), packed)
        packed_factor = jnp.where(here, pltpu.roll(scaled, 2 * cell + 1, 1), packed_factor)
    r.own_ends[0, rows, :] = jnp.where(core == 0, packed, pltpu.roll(packed, 64, 1))
    r.own_ends[1, rows, :] = jnp.where(core == 0, packed_factor, pltpu.roll(packed_factor, 64, 1))


def merge(r, core, tile):
    rows = row_block(tile)
    low = lane_at() < 64
    ours = jnp.where(core == 0, jnp.where(low, 1, 0), jnp.where(low, 0, 1)) == 1
    held = pl.ds(pl.multiple_of(core * ROWS + tile * 8, 8), 8)
    r.ends[0, rows, :] = jnp.where(ours, r.own_ends[0, held, :], r.paired_ends[0, rows, :])
    r.factor_ends[rows, :] = jnp.where(ours, r.own_ends[1, held, :], r.paired_ends[1, rows, :])
    for side in range(2):
        r.near_ends[0, side, rows, :] = jnp.where(
            low, r.halves[side, 0, 0, rows, :], r.halves[side, 1, 0, rows, :]
        )
        r.near_factor[side, rows, :] = jnp.where(
            low, r.halves[side, 0, 1, rows, :], r.halves[side, 1, 1, rows, :]
        )


def border_of(r, core, low_gz, high_gz, step, tile):
    rows = row_block(tile)
    rate = (2.0 * lengthwise_ratio) / twice_number(core, tile)
    even = lax.rem(lane_at(), 2) == 0
    inside = jnp.where(even, high_gz, low_gz)
    ours = r.ends[step, rows, :]
    near = jnp.where(
        even,
        pltpu.roll(r.near_ends[step, 0, rows, :], LANES - 1, 1),
        pltpu.roll(r.near_ends[step, 1, rows, :], 1, 1),
    )
    near_factor = jnp.where(
        even,
        pltpu.roll(r.near_factor[0, rows, :], LANES - 1, 1),
        pltpu.roll(r.near_factor[1, rows, :], 1, 1),
    )
    our_k = conduct(ours, r.factor_ends[rows, :])
    near_k = conduct(near, near_factor)
    return rate * inside * our_k * near_k / (our_k + near_k) * (near - ours)


def explicit(number, field, factor, beyond, supply, rows, cells, store):
    rate = (2.0 * lengthwise_ratio) / number
    last = lane_at() == LANES - 1
    for group in range(0, cells, GROUP):
        at = range(group, group + GROUP)
        here = [field[cell, rows, :] for cell in at]
        k = [conduct(x, factor[cell, rows, :]) for cell, x in zip(at, here)]
        above = [pltpu.roll(x, LANES - 1, 1) for x in here]
        if beyond is None:
            k_above = [pltpu.roll(x, LANES - 1, 1) for x in k]
        else:
            k_above = [conduct(x, beyond[cell, rows, :]) for cell, x in zip(at, above)]
        flux = [
            jnp.where(last, 0.0, rate * k[i] * k_above[i] / (k[i] + k_above[i]) * (above[i] - here[i]))
            for i in range(GROUP)
        ]
        below = [pltpu.roll(x, 1, 1) for x in flux]
        for i, cell in enumerate(at):
            store(cell, here[i] + (flux[i] - below[i]) + supply[cell, rows, :])


def explicit_first(r, target, base, row_shift, tile):
    rows = row_block(tile)
    placed = pl.ds(pl.multiple_of(tile * 8 - row_shift, 8), 8)

    def store(cell, value):
        target[base + cell, placed, :] = value

    explicit(first_rows(tile), r.own_field, r.scaled, None, r.own_supply, rows, HALF, store)


def explicit_later(r, core, tile):
    rows = row_block(tile)

    def store(cell, value):
        r.raw[cell, rows, :] = value

    explicit(
        twice_number(core, tile), r.field, r.factor, r.beyond, r.supply, rows, CELLS, store
    )


def shift_factor(r, tile):
    rows = row_block(tile)
    for cell in range(CELLS):
        r.beyond[cell, rows, :] = pltpu.roll(r.factor[cell, rows, :], LANES - 1, 1)


def reduce_tile(r, border, turn, tile):
    rows = row_block(tile)
    lane = lane_at()
    rim = jnp.logical_or(lane == 0, lane == LANES - 1)

    def k_of(cell):
        if border is None:
            return conduct(r.field[cell, rows, :], r.factor[cell, rows, :]), r.goal[cell, rows, :]
        edge = jnp.where(rim, pltpu.roll(border, LANES - 1 - 2 * cell, 1), 0.0)
        total = r.raw[cell, rows, :] + edge
        r.goal[cell, rows, :] = total
        return conduct(total, r.factor[cell, rows, :]), total

    heads = {start: k_of(start) for start in STARTS}
    first_k = heads[0][0]
    state = []
    for start in STARTS:
        after, after_side = k_of(start + 1)
        head_k = heads[start][0]
        link = head_k * after / (head_k + after)
        if start == 0:
            head_ground = jnp.ones((8, LANES), jnp.float32)
            head_side = heads[0][1]
        else:
            head_ground = jnp.zeros((8, LANES), jnp.float32)
            head_side = jnp.zeros((8, LANES), jnp.float32)
        state.append(
            (jnp.ones((8, LANES), jnp.float32), link, after_side, head_ground, head_side, after)
        )
    last_k = None
    for offset in range(1, 16):
        for chain, (start, end) in enumerate(zip(STARTS, ENDS)):
            cell = start + offset
            if cell >= end:
                continue
            ground, link, side, head_ground, head_side, k = state[chain]
            after, after_side = heads[cell + 1] if cell + 1 in heads else k_of(cell + 1)
            both = k + after
            product = k * after
            inverse = 1.0 / ((ground + link) * both + product)
            own = both * inverse
            ahead = product * inverse
            back = link * own
            r.to_next[cell, rows, :] = ahead
            r.to_sep[cell, rows, :] = back
            r.base[cell, rows, :] = side * own
            state[chain] = (
                1.0 + ground * ahead,
                link * ahead,
                after_side + side * ahead,
                head_ground + ground * back,
                head_side + side * back,
                after,
            )
            if cell + 1 == CELLS - 1:
                last_k = after
    ground_16 = state[0][0] + state[1][3]
    side_16 = state[0][2] + state[1][4]
    ground_32 = state[1][0] + state[2][3]
    side_32 = state[1][2] + state[2][4]
    ground_48 = state[2][0] + state[3][3]
    side_48 = state[2][2] + state[3][4]
    ground_0, side_0 = state[0][3], state[0][4]
    ground_63, side_63 = state[3][0], state[3][2]
    links = [part[1] for part in state]

    left, right, own = eliminate(ground_16, links[0], links[1], side_16)
    r.to_sep[16, rows, :] = left
    r.to_next[16, rows, :] = right
    r.base[16, rows, :] = own
    ground_0 += ground_16 * left
    side_0 += side_16 * left
    ground_32 += ground_16 * right
    side_32 += side_16 * right
    link_low = links[0] * right

    left, right, own = eliminate(ground_48, links[2], links[3], side_48)
    r.to_sep[48, rows, :] = left
    r.to_next[48, rows, :] = right
    r.base[48, rows, :] = own
    ground_32 += ground_48 * left
    side_32 += side_48 * left
    ground_63 += ground_48 * right
    side_63 += side_48 * right
    link_high = links[2] * right

    left, right, own = eliminate(ground_32, link_low, link_high, side_32)
    r.to_sep[32, rows, :] = left
    r.to_next[32, rows, :] = right
    r.base[32, rows, :] = own
    ground_0 += ground_32 * left
    side_0 += side_32 * left
    ground_63 += ground_32 * right
    side_63 += side_32 * right
    link = link_low * right

    to_face, to_last, own = eliminate(ground_0, first_k, link, side_0)
    r.to_sep[0, rows, :] = to_face
    r.to_next[0, rows, :] = to_last
    r.base[0, rows, :] = own
    ground_low = ground_0 * to_face
    side_low = side_0 * to_face
    ground_63 += ground_0 * to_last
    side_63 += side_0 * to_last
    link = first_k * to_last

    to_low, to_high, own = eliminate(ground_63, link, last_k, side_63)
    r.to_sep[63, rows, :] = to_low
    r.to_next[63, rows, :] = to_high
    r.base[63, rows, :] = own
    ground_low += ground_63 * to_low
    side_low += side_63 * to_low
    link = link * to_high
    faces = (link, ground_low, ground_63 * to_high, side_low, side_63 * to_high)
    for at, value in enumerate(faces):
        r.packet[turn, tile, at] = value


def spread_tile(r, turn, pack_to, tile):
    rows = row_block(tile)
    low_face = r.returned[turn, tile, 0]
    high_face = r.returned[turn, tile, 1]
    lane_pair = lane_at() // 2
    packed = [jnp.zeros((8, LANES), jnp.float32)]

    def value(cell, sep, following):
        return (
            r.base[cell, rows, :]
            + r.to_sep[cell, rows, :] * sep
            + r.to_next[cell, rows, :] * following
        )

    def keep(cell, x):
        r.field[cell, rows, :] = x
        if pack_to is not None:
            packed[0] = jnp.where(lane_pair == cell, pltpu.roll(x, 2 * cell + 1, 1), packed[0])

    x_last = value(63, low_face, high_face)
    x_first = value(0, low_face, x_last)
    x_32 = value(32, x_first, x_last)
    x_16 = value(16, x_first, x_32)
    x_48 = value(48, x_32, x_last)
    seps = {0: x_first, 16: x_16, 32: x_32, 48: x_48, 63: x_last}
    for cell, x in seps.items():
        keep(cell, x)
    later = [seps[end] for end in ENDS]
    for offset in range(15, 0, -1):
        for chain, (start, end) in enumerate(zip(STARTS, ENDS)):
            cell = start + offset
            if cell >= end:
                continue
            later[chain] = value(cell, seps[start], later[chain])
            keep(cell, later[chain])
    if pack_to is not None:
        r.ends[pack_to, rows, :] = packed[0]


def close_ring(r, turn, chunk):
    parts = [[r.gathered[turn, chunk, member, at] for at in range(VALUES)] for member in range(TILES)]
    count = TILES
    ground = [parts[at][1] + parts[at - 1][2] for at in range(count)]
    side = [parts[at][3] + parts[at - 1][4] for at in range(count)]
    links = [parts[at - 1][0] for at in range(count)]
    undo = []
    nodes = list(range(count))
    while len(nodes) > 2:
        size = len(nodes)
        kept_links = []
        for at in range(1, size, 2):
            node, low, high = nodes[at], nodes[at - 1], nodes[(at + 1) % size]
            to_low, to_high, own = eliminate(ground[node], links[at], links[(at + 1) % size], side[node])
            undo.append((node, low, high, to_low, to_high, own))
            ground[low] = ground[low] + ground[node] * to_low
            side[low] = side[low] + side[node] * to_low
            ground[high] = ground[high] + ground[node] * to_high
            side[high] = side[high] + side[node] * to_high
            kept_links.append(links[at] * to_high)
        nodes = nodes[::2]
        links = kept_links[-1:] + kept_links[:-1]
    low, high = nodes
    link = links[0] + links[1]
    inverse = 1.0 / (ground[high] + link)
    to_low = link * inverse
    x = [None] * count
    x[low] = (side[low] + side[high] * to_low) / (ground[low] + ground[high] * to_low)
    x[high] = side[high] * inverse + to_low * x[low]
    for node, low, high, to_low, to_high, own in reversed(undo):
        x[node] = own + to_low * x[low] + to_high * x[high]
    for member in range(count):
        r.answer[turn, chunk, member, 0] = x[member]
        r.answer[turn, chunk, member, 1] = x[(member + 1) % count]


NAMES = (
    "field", "factor", "beyond", "supply", "raw", "goal", "to_sep", "to_next", "base",
    "own_field", "own_factor", "own_supply", "scaled", "stage",
    "own_ends", "paired_ends", "halves", "ends", "factor_ends", "near_ends", "near_factor",
    "packet", "gathered", "answer", "returned",
    "load_sem", "move_sem", "swap_send", "swap_recv", "first_send", "first_recv",
    "halo_send", "halo_recv", "packet_send", "packet_recv", "answer_send", "answer_recv",
    "out_sem", "out_send", "out_recv",
)


def kernel(warmth_hbm, factor_hbm, supply_hbm, out_hbm, *refs):
    r = types.SimpleNamespace(**dict(zip(NAMES, refs)))
    az = lax.axis_index("az")
    gz = lax.axis_index("gz")
    core = lax.rem(az, 2)
    chip = az // 2
    sibling = az + 1 - 2 * core
    gz_count = lax.axis_size("gz")
    across = gz + 1 - 2 * lax.rem(gz, 2)
    gz_up = lax.rem(gz + 1, gz_count)
    gz_down = lax.rem(gz + gz_count - 1, gz_count)
    other = lax.rem(gz + gz_count - 1 + 2 * lax.rem(gz, 2), gz_count)
    low_gz = jnp.where(gz > 0, 1.0, 0.0)
    high_gz = jnp.where(gz < gz_count - 1, 1.0, 0.0)

    barrier = pltpu.get_barrier_semaphore()
    for member in range(TILES):
        pl.semaphore_signal(
            barrier, inc=1, device_id=(2 * member + 1 - core, across), device_id_type=MESH
        )
    for where in ((sibling, gz), (az, across), (az, other), (sibling, other)):
        pl.semaphore_signal(barrier, inc=1, device_id=where, device_id_type=MESH)

    def for_range(low, high, work):
        def one(at, carry):
            work(at)
            return carry

        lax.fori_loop(low, high, one, 0)

    def remote(source, target, send_sem, recv_sem, where):
        return pltpu.make_async_remote_copy(
            src_ref=source, dst_ref=target, send_sem=send_sem, recv_sem=recv_sem,
            device_id=where, device_id_type=MESH,
        )

    def wait_for(ref, sem):
        pltpu.make_async_copy(ref, ref, sem).wait()

    loads = ((warmth_hbm, r.own_field), (factor_hbm, r.own_factor), (supply_hbm, r.own_supply))

    def load(arrays, cell):
        for at in arrays:
            source, target = loads[at]
            pltpu.make_async_copy(source.at[:, cell], target.at[cell], r.load_sem.at[at]).start()

    for_range(0, HALF, functools.partial(load, (0, 1)))
    for_range(0, HALF, functools.partial(load, (2,)))
    for at in range(2):
        wait_for(loads[at][1], r.load_sem.at[at])

    own_rows = pl.ds(core * ROWS, ROWS)
    sent_rows = pl.ds((1 - core) * ROWS, ROWS)
    own_cells = pl.ds(core * HALF, HALF)
    sent_tile = (1 - core) * TILES
    own_tile = core * TILES

    for_range(sent_tile, sent_tile + TILES, functools.partial(prepare, r, core))
    pl.semaphore_wait(barrier, TILES + 4)
    factor_swap = remote(
        r.scaled.at[:, sent_rows], r.factor.at[own_cells],
        r.swap_send.at[0], r.swap_recv.at[0], (sibling, gz),
    )
    factor_swap.start()
    for_range(own_tile, own_tile + TILES, functools.partial(prepare, r, core))
    factor_move = pltpu.make_async_copy(
        r.scaled.at[:, own_rows], r.factor.at[own_cells], r.move_sem.at[0]
    )
    factor_move.start()
    firsts = []
    for side, where in enumerate((gz_down, gz_up)):
        for same in range(2):
            firsts.append(
                remote(
                    r.own_ends.at[:, own_rows if same else sent_rows],
                    r.halves.at[side, core],
                    r.first_send.at[2 * side + same],
                    r.first_recv.at[2 * side + core],
                    (az if same else sibling, where),
                )
            )
    firsts.append(
        remote(
            r.own_ends.at[:, sent_rows], r.paired_ends,
            r.first_send.at[4], r.first_recv.at[4], (sibling, gz),
        )
    )
    for copy in firsts:
        copy.start()
    wait_for(r.own_supply, r.load_sem.at[2])

    goal_swaps = []
    for chunk in range(2):
        low = sent_tile + PART * chunk
        for_range(
            low, low + PART,
            functools.partial(explicit_first, r, r.stage, 0, sent_tile * 8),
        )
        rows = pl.ds(PART * 8 * chunk, PART * 8)
        goal_swaps.append(
            remote(
                r.stage.at[:, rows], r.raw.at[own_cells, rows],
                r.swap_send.at[1 + chunk], r.swap_recv.at[1 + chunk], (sibling, gz),
            )
        )
        goal_swaps[-1].start()
    supply_swap = remote(
        r.own_supply.at[:, sent_rows], r.supply.at[own_cells],
        r.swap_send.at[3], r.swap_recv.at[3], (sibling, gz),
    )
    supply_move = pltpu.make_async_copy(
        r.own_supply.at[:, own_rows], r.supply.at[own_cells], r.move_sem.at[1]
    )
    for_range(
        own_tile, own_tile + TILES,
        functools.partial(explicit_first, r, r.raw, core * HALF, own_tile * 8),
    )
    for side in range(2):
        for source in range(2):
            wait_for(r.halves.at[side, source], r.first_recv.at[2 * side + source])
    wait_for(r.paired_ends, r.first_recv.at[4])
    for_range(0, TILES, functools.partial(merge, r, core))
    factor_move.wait()
    factor_swap.wait_recv()

    y_at = lax.rem(chip, 4)

    def wrap(shift):
        return jnp.where(y_at + shift >= 4, y_at + shift - 4, y_at + shift)

    seats = [wrap(2), wrap(1), wrap(3), y_at]

    layer = lax.rem(gz, 2)
    solves = chip // 4 == 1 - layer

    def ordered(at):
        first = jnp.where(at == 0, seats[0], seats[1])
        return jnp.where(at < 2, first, jnp.where(at == 2, seats[2], seats[3]))

    def forward(step, picard, chunk):
        turn = PICARD * step + picard

        def work(at):
            seat = ordered(at)
            tile = PART * chunk + seat
            border = None if picard else border_of(r, core, low_gz, high_gz, step, tile)
            reduce_tile(r, border, turn, tile)
            remote(
                r.packet.at[turn, tile], r.gathered.at[turn, chunk, chip],
                r.packet_send.at[turn], r.packet_recv.at[turn, chunk],
                (2 * (4 * layer + seat) + 1 - core, across),
            ).start()

        for_range(0, PART, work)

    def solve(turn):
        @pl.when(solves)
        def _():
            for chunk in range(2):
                wait_for(r.gathered.at[turn, chunk], r.packet_recv.at[turn, chunk])
                close_ring(r, turn, chunk)
                tile = PART * chunk + y_at
                for seat in seats:
                    for half in range(2):
                        member = seat + 4 * half
                        remote(
                            r.answer.at[turn, chunk, member], r.returned.at[turn, tile],
                            r.answer_send.at[turn], r.answer_recv.at[turn, tile],
                            (2 * member + 1 - core, across),
                        ).start()

    def backward(turn, chunk, pack_to):
        def work(at):
            tile = PART * chunk + ordered(PART - 1 - at)
            wait_for(r.returned.at[turn, tile], r.answer_recv.at[turn, tile])
            spread_tile(r, turn, pack_to, tile)

        for_range(0, PART, work)

    def unload(chunk):
        rows = pl.ds(PART * 8 * chunk, PART * 8)
        placed = pl.ds(core * ROWS + PART * 8 * chunk, PART * 8)

        def to_sibling(cell):
            remote(
                r.field.at[(1 - core) * HALF + cell, rows], out_hbm.at[placed, cell],
                r.out_send, r.out_recv, (sibling, gz),
            ).start()

        def to_own(cell):
            pltpu.make_async_copy(
                r.field.at[core * HALF + cell, rows], out_hbm.at[placed, cell], r.out_sem
            ).start()

        for_range(0, HALF, to_sibling)
        for_range(0, HALF, to_own)

    halos = [[], []]
    for step in range(STEPS):
        for chunk in range(2):
            rows = pl.ds(PART * 8 * chunk, PART * 8)
            if step == 0:
                goal_swaps[chunk].wait_recv()
            else:
                low = PART * chunk
                for_range(low, low + PART, functools.partial(explicit_later, r, core))
                for copy in halos[chunk]:
                    copy.wait()
            forward(step, 0, chunk)
        if step == 0:
            supply_swap.start()
            supply_move.start()
        for picard in range(PICARD):
            turn = PICARD * step + picard
            final = picard == PICARD - 1
            solve(turn)
            if turn == 0:
                for_range(0, TILES, functools.partial(shift_factor, r))
            for chunk in range(2):
                last = step == STEPS - 1
                backward(turn, chunk, step + 1 if final and not last else None)
                if not final:
                    forward(step, picard + 1, chunk)
                elif last:
                    unload(chunk)
                else:
                    rows = pl.ds(PART * 8 * chunk, PART * 8)
                    for side, where in enumerate((gz_down, gz_up)):
                        copy = remote(
                            r.ends.at[step + 1, rows], r.near_ends.at[step + 1, side, rows],
                            r.halo_send.at[chunk, side], r.halo_recv.at[chunk, side],
                            (az, where),
                        )
                        copy.start()
                        halos[chunk].append(copy)
        if step == 0:
            supply_swap.wait_recv()
            supply_move.wait()

    for copy in [factor_swap, supply_swap] + goal_swaps + firsts:
        copy.wait_send()
    for turn in range(STEPS * PICARD):
        wait_for(r.packet.at[turn], r.packet_send.at[turn])

    @pl.when(solves)
    def _():
        for turn in range(STEPS * PICARD):
            wait_for(r.answer.at[turn], r.answer_send.at[turn])

    whole = r.field.at[pl.ds(0, HALF)]
    wait_for(whole, r.out_sem)
    wait_for(whole, r.out_send)
    wait_for(whole, r.out_recv)


def shards(starting_warmth, volume_transfer_multiplier, energy_supply_history):
    def real(*shape):
        return pltpu.VMEM(shape + (LANES,), jnp.float32)

    cells = real(CELLS, ROWS)
    own = real(HALF, 2 * ROWS)
    dma = pltpu.SemaphoreType.DMA
    turns = STEPS * PICARD
    anywhere = pl.BlockSpec(memory_space=pltpu.HBM)
    return pl.pallas_call(
        kernel,
        out_shape=jax.ShapeDtypeStruct(starting_warmth.shape, jnp.float32),
        in_specs=[anywhere] * 3,
        out_specs=anywhere,
        scratch_shapes=[cells] * 9 + [own] * 4 + [
            real(HALF, ROWS),
            real(2, 2 * ROWS), real(2, ROWS), real(2, 2, 2, ROWS), real(STEPS, ROWS),
            real(ROWS), real(STEPS, 2, ROWS), real(2, ROWS),
            real(turns, TILES, VALUES, 8), real(turns, 2, TILES, VALUES, 8),
            real(turns, 2, TILES, 2, 8), real(turns, TILES, 2, 8),
            dma((3,)), dma((2,)), dma((4,)), dma((4,)), dma((5,)), dma((5,)),
            dma((2, 2)), dma((2, 2)),
            dma((turns,)), dma((turns, 2)), dma((turns,)), dma((turns, TILES)),
            dma, dma, dma,
        ],
        compiler_params=pltpu.CompilerParams(
            collective_id=0, has_side_effects=True, vmem_limit_bytes=60 * 1024 * 1024
        ),
        name="annulus",
    )(starting_warmth, volume_transfer_multiplier, energy_supply_history)


def solution(mesh):
    placed = (P(None, "az", "gz"), P(None, "az", "gz"), P(None, "az", "gz"))
    return jax.shard_map(
        shards, mesh=mesh, in_specs=placed, out_specs=P(None, "az", "gz"), check_vma=False
    )
```
